256 devices in a mesh: sub: 256 (over z, y, x, core).
Axes of the slice: x: 4, y: 4, z: 8, core: 2. Of those that a mesh axis runs over, the one named last changes fastest.
Arguments:
- stiffness: float32 [256, 1024, 1024], P('sub'), as said below
- neumann_inv: float32 [256, 1024, 1024], P('sub'), as said below
- coarse_basis: float32 [256, 16, 1024], P('sub'), may hold values from -0.375 to 0.375
- coarse_inv: float32 [4096, 4096], P('sub'), as said below
- loads: float32 [256, 64, 1024], P('sub'), may hold values from -6 to 6
- face_index: int32 [256, 4, 128], P('sub'), may hold values from 0 to 1023, as said below
- face_len: int32 [256, 4], P('sub'), may hold values from 0 to 128, as said below
Outputs:
- solution: float32 [256, 64, 1024], P('sub')
- residual: float32 [256, 64, 1024], P('sub')
The draws below stay inside these ranges and needn't reach their ends.
Inputs may be any that keep to these rules, and one draw needn't show every extreme that they name: `face_index`: within one subdomain all 512 entries are distinct. `face_len`: A block without a neighbour has length 0; paired blocks of two neighbours have equal length; some block has length 128. `stiffness`: each matrix is exactly symmetric and positive definite. `neumann_inv`: each matrix is exactly symmetric and positive definite. `coarse_inv`: the matrix is exactly symmetric and positive definite.
All inputs are finite; a program needn't handle non-finite values.
Results may differ from the reference program's by a relative error of at most 0.00022.
Values sent between devices are 32-bit elements; how exact they have to be, the bound alone decides.
A program may use at most 64 MiB of HBM per device.

```python
import jax
import jax.numpy as jnp
from jax import lax

NDOF = 1024
CASES = 64
FACE = 128
CYCLE = 16
PRIMAL = 16
ITERS = 4
SUBS = 256
COARSE = 4096


def spd_draw(key, count, order):
    noise = jax.random.normal(key, (count, order, order), jnp.float32)
    sym = (noise + jnp.swapaxes(noise, 1, 2)) / (2.0 * jnp.sqrt(jnp.float32(order)))
    return sym + 2.0 * jnp.eye(order, dtype=jnp.float32)[None]


def draw_stiffness(key, part):
    return spd_draw(jax.random.fold_in(key, 11), SUBS, NDOF)


def draw_neumann_inv(key, part):
    return spd_draw(jax.random.fold_in(key, 12), SUBS, NDOF)


def draw_coarse_inv(key, part):
    return spd_draw(jax.random.fold_in(key, 13), 1, COARSE)[0]


def draw_face_index(key, part):
    keys = jax.random.split(jax.random.fold_in(key, 14), SUBS)
    picks = jax.vmap(lambda one: jax.random.permutation(one, NDOF)[:4 * FACE])(keys)
    return picks.reshape(SUBS, 4, FACE).astype(jnp.int32)


def draw_face_len(key, part):
    key_h = jax.random.fold_in(key, 15)
    key_v = jax.random.fold_in(key, 16)
    across = jax.random.randint(key_h, (SUBS,), FACE // 3, FACE + 1).astype(jnp.int32)
    across = across.at[0].set(FACE)
    along = jax.random.randint(key_v, (SUBS,), FACE // 3, FACE + 1).astype(jnp.int32)
    position = jnp.arange(SUBS, dtype=jnp.int32)
    rowpos = position // CYCLE
    east = jnp.where(position == SUBS - 1, 0, across)
    north = jnp.where(rowpos == SUBS // CYCLE - 1, 0, along)
    west = jnp.roll(east, 1)
    south = jnp.roll(north, CYCLE)
    return jnp.stack([west, east, south, north], axis=1).astype(jnp.int32)


def block_scale(own_key, extent, cuts, smallest, high):
    loudness = 1.0
    for axis_at, blocks in cuts:
        heights = jax.random.uniform(jax.random.fold_in(jax.random.fold_in(own_key, 6), axis_at), (blocks,), jnp.float32, smallest / len(cuts), high / len(cuts))
        loudness = loudness * jnp.repeat(jnp.exp(heights), extent[axis_at] // blocks).reshape((-1,) + (1,) * (len(extent) - 1 - axis_at))
    return loudness


def normal_values(key, dims, scale, most, cuts=(), kind=jnp.bfloat16):
    result = jax.random.normal(key, dims, jnp.float32) * scale
    if len(cuts) > 0:
        result = block_scale(key, dims, cuts, -0.22, 0.18) * result
    return jnp.clip(result, min=-most, max=most).astype(kind)


def setup_inputs(seed: int = 0) -> dict:
    splits = jax.random.split(jax.random.key(seed), 8)
    return {
        "stiffness": draw_stiffness(jax.random.fold_in(splits[7], 71), 0),
        "neumann_inv": draw_neumann_inv(jax.random.fold_in(splits[7], 71), 0),
        "coarse_basis": normal_values(splits[2], (SUBS, PRIMAL, NDOF), (2.0 / NDOF ** 0.5), 0.375, ((0, 256),), jnp.float32),
        "coarse_inv": draw_coarse_inv(jax.random.fold_in(splits[7], 71), 0),
        "loads": normal_values(splits[4], (SUBS, CASES, NDOF), 1.0, 6.0, ((0, 256),), jnp.float32),
        "face_index": draw_face_index(jax.random.fold_in(splits[7], 71), 0),
        "face_len": draw_face_len(jax.random.fold_in(splits[7], 71), 0),
    }


HIGH = lax.Precision.HIGHEST


def assemble(local_vals, face_slots, live_slots):
    face_vals = jax.vmap(lambda loc, slot: jnp.take(loc, slot, axis=1))(local_vals, face_slots)
    face_vals = face_vals * live_slots[:, None, :]
    subs, cases = face_vals.shape[0], face_vals.shape[1]
    blocks = face_vals.reshape(subs, cases, 4, -1)
    west_in = jnp.roll(blocks[:, :, 1], 1, axis=0)
    east_in = jnp.roll(blocks[:, :, 0], -1, axis=0)
    south_in = jnp.roll(blocks[:, :, 3], CYCLE, axis=0)
    north_in = jnp.roll(blocks[:, :, 2], -CYCLE, axis=0)
    incoming = jnp.stack([west_in, east_in, south_in, north_in], axis=2).reshape(subs, cases, -1)
    incoming = incoming * live_slots[:, None, :]
    return jax.vmap(lambda loc, slot, extra: loc.at[:, slot].add(extra))(local_vals, face_slots, incoming)


def reference(stiffness, neumann_inv, coarse_basis, coarse_inv, loads, face_index, face_len):
    subs = stiffness.shape[0]
    width = face_index.shape[2]
    face_slots = face_index.reshape(subs, -1).astype(jnp.int32)
    slot_pos = jnp.arange(width, dtype=jnp.int32)
    live_slots = (slot_pos[None, None, :] < face_len[:, :, None]).astype(jnp.float32).reshape(subs, -1)
    counts = jax.vmap(lambda slot, live: jnp.ones((NDOF,), jnp.float32).at[slot].add(live))(face_slots, live_slots)
    weight = 1.0 / counts

    def inner(left, right):
        return jnp.sum(left * right * weight[:, None, :], axis=(0, 2))

    def apply_op(field):
        return assemble(jnp.einsum("skn,snm->skm", field, stiffness, precision=HIGH), face_slots, live_slots)

    def precond(resid):
        scaled = weight[:, None, :] * resid
        local_sol = jnp.einsum("skn,snm->skm", scaled, neumann_inv, precision=HIGH)
        coarse_res = jnp.einsum("scn,skn->sck", coarse_basis, scaled, precision=HIGH)
        coarse_sol = jnp.dot(coarse_inv, coarse_res.reshape(-1, coarse_res.shape[2]), precision=HIGH)
        coarse_sol = coarse_sol.reshape(coarse_res.shape)
        local_sol = local_sol + jnp.einsum("sck,scn->skn", coarse_sol, coarse_basis, precision=HIGH)
        return assemble(weight[:, None, :] * local_sol, face_slots, live_slots)

    residual = assemble(loads, face_slots, live_slots)
    solution = jnp.zeros_like(residual)
    precond_res = precond(residual)
    direction = precond_res
    rz_now = inner(residual, precond_res)
    for step in range(ITERS):
        image = apply_op(direction)
        alpha = rz_now / inner(direction, image)
        solution = solution + alpha[None, :, None] * direction
        residual = residual - alpha[None, :, None] * image
        if step + 1 < ITERS:
            precond_res = precond(residual)
            rz_next = inner(residual, precond_res)
            direction = precond_res + (rz_next / rz_now)[None, :, None] * direction
            rz_now = rz_next
    return solution, residual
```

```python
import functools

import jax
import jax.numpy as jnp
from jax import lax
from jax.experimental import pallas as pl
from jax.experimental.pallas import tpu as pltpu
from jax.sharding import PartitionSpec as P

CYCLE = 16
ITERS = 4
LINE = 8
ROWS = 4
MESH = pl.DeviceIdType.MESH
F32 = jnp.float32
BF16 = jnp.bfloat16


def halves(value):
    high = value.astype(BF16)
    return high, (value - high.astype(F32)).astype(BF16)


def thirds(value):
    high = value.astype(BF16)
    rest = value - high.astype(F32)
    mid = rest.astype(BF16)
    return high, mid, (rest - mid.astype(F32)).astype(BF16)


def dot(left, right):
    return jnp.dot(left, right, preferred_element_type=F32)


def dot_nt(left, right):
    return lax.dot_general(left, right, (((1,), (1,)), ((), ())), preferred_element_type=F32)


def iota(shape, dim):
    return lax.broadcasted_iota(jnp.int32, shape, dim)


def three(parts, cases):
    return parts[:cases] + parts[cases:2 * cases] + parts[2 * cases:]


def arrange(
    stiff_ref, neum_ref, basis_ref, loads_ref, index_ref,
    perm, neum_hi, neum_lo, stiff_hi, stiff_lo, basis_out, loads_out, turned_hi, turned_lo,
):
    cases, ndof = loads_ref.shape[1:]
    faces, width = index_ref.shape[1:]
    shared = faces * width

    columns = jnp.concatenate([index_ref[0].astype(F32), jnp.zeros((8 - faces, width), F32)], axis=0).T
    for block in range(faces):
        hit = columns[:, block:block + 1].astype(jnp.int32) == iota((width, ndof), 1)
        perm[block * width:(block + 1) * width, :] = jnp.where(hit, 1.0, 0.0).astype(BF16)
    taken = dot(jnp.ones((16, shared), BF16), perm[:shared, :])[:8]
    free = (1.0 - taken).astype(BF16)
    rank = jnp.zeros((8, ndof), F32)
    for block in range(0, ndof, 128):
        before = jnp.where(iota((128, ndof), 0) + block < iota((128, ndof), 1), 1.0, 0.0).astype(BF16)
        rank = rank + dot(free[:, block:block + 128], before)
    place = jnp.where(taken[:1] > 0.5, -1.0, rank[:1]).astype(jnp.int32)
    for block in range(0, ndof - shared, 128):
        hit = place == iota((128, ndof), 0) + block
        perm[shared + block:shared + block + 128, :] = jnp.where(hit, 1.0, 0.0).astype(BF16)

    loads_out[...] = three(dot_nt(jnp.concatenate(thirds(loads_ref[0]), axis=0), perm[...]), cases)
    basis = three(dot_nt(jnp.concatenate(thirds(basis_ref[0]), axis=0), perm[...]), 16)
    basis_hi, basis_lo = halves(basis)
    basis_out[...] = jnp.concatenate(
        [basis_hi, basis_lo, basis_hi, basis_lo, basis_hi, jnp.zeros_like(basis_hi)], axis=0
    )

    tall = 256
    for raw, out_hi, out_lo in ((neum_ref, neum_hi, neum_lo), (stiff_ref, stiff_hi, stiff_lo)):
        def turn(step, carry, raw=raw):
            here = pl.ds(pl.multiple_of(step * tall, tall), tall)
            high, low = halves(raw[0, here, :])
            both = dot_nt(jnp.concatenate([high, low], axis=0), perm[...]).astype(BF16)
            turned_hi[here, :] = both[:tall]
            turned_lo[here, :] = both[tall:]
            return carry

        def settle(step, carry, out_hi=out_hi, out_lo=out_lo):
            here = pl.ds(pl.multiple_of(step * tall, tall), tall)
            pick = perm[here, :]
            out_hi[here, :] = dot(pick, turned_hi[...]).astype(BF16)
            out_lo[here, :] = dot(pick, turned_lo[...]).astype(BF16)
            return carry

        lax.fori_loop(0, ndof // tall, turn, 0)
        lax.fori_loop(0, ndof // tall, settle, 0)


def restore(sol_ref, res_ref, perm, sol_out, res_out):
    cases = sol_ref.shape[0]
    sol_out[0] = three(dot(jnp.concatenate(thirds(sol_ref[...]), axis=0), perm[...]), cases)
    res_out[0] = three(dot(jnp.concatenate(thirds(res_ref[...]), axis=0), perm[...]), cases)


def kernel(
    sizes, cycle, neum_hi, neum_lo, stiff_hi, stiff_lo, basis, loads_ref, coarse_hbm, len_ref, sol_ref, res_ref,
    coarse_raw, coarse_cat, image_ref, direction_ref, local_ref, scalars, coarse_state, face_out, face_in,
    gather, gather_own, spread, spread_out, sums, sums_own, mids, mids_own, tops, tops_own,
    load_sem, face_send, face_recv, line_send, line_recv, rows_send, rows_recv, deep_send, deep_recv,
):
    planes, rows, line = sizes
    subs, plane = planes * rows * line, rows * line
    cases, ndof = loads_ref.shape
    faces, width = face_in.shape[1], face_in.shape[3]
    shared = faces * width
    wide = 2 * cases
    me = lax.axis_index("sub")
    deep, col = me // plane, lax.rem(me, plane)
    row, spot = col // line, lax.rem(col, line)
    left_half = iota((1, wide), 1) < cases

    def flip(value):
        return pltpu.roll(value, cases, axis=value.ndim - 1)

    sides = (
        lax.rem(me + subs - 1, subs), lax.rem(me + 1, subs),
        lax.rem(me + subs - cycle, subs), lax.rem(me + cycle, subs),
    )
    line_others = [(me - spot + at, at) for at in [lax.rem(spot + step, line) for step in range(1, line)]]
    rows_others = [(me + (at - row) * line, at) for at in [lax.rem(row + step, rows) for step in range(1, rows)]]
    deep_others = [(me + (at - deep) * plane, at) for at in [lax.rem(deep + step, planes) for step in range(1, planes)]]

    def remote(src, dst, send, recv, peer):
        return pltpu.make_async_remote_copy(
            src_ref=src, dst_ref=dst, send_sem=send, recv_sem=recv, device_id=(peer,), device_id_type=MESH
        )

    def coarse_cols(at):
        return pl.ds(pl.multiple_of(at * (plane * 16), plane * 16), plane * 16)

    load_coarse = pltpu.make_async_copy(coarse_hbm.at[:, coarse_cols(deep)], coarse_raw.at[deep], load_sem)
    load_coarse.start()

    barrier = pltpu.get_barrier_semaphore()
    everyone = [peer for peer, _ in line_others + rows_others + deep_others] + list(sides)
    for peer in everyone:
        pl.semaphore_signal(barrier, inc=1, device_id=(peer,), device_id_type=MESH)
    live = jnp.concatenate([iota((1, width), 1) < len_ref[0, block] for block in range(faces)], axis=1)
    weight = jnp.concatenate([jnp.where(live, 0.5, 1.0), jnp.ones((1, ndof - shared), F32)], axis=1)
    pl.semaphore_wait(barrier, len(everyone))

    def face_copy(kind, block):
        pair = block ^ 1
        return remote(
            face_out.at[kind, block], face_in.at[kind, pair], face_send.at[kind, block], face_recv.at[kind, pair],
            sides[block],
        )

    def start_faces(kind, value):
        for block in range(faces):
            face_out[kind, block] = value[:, block * width:(block + 1) * width]
        for block in range(faces):
            face_copy(kind, block).start()

    def wait_faces(kind):
        for block in range(faces):
            face_copy(kind, block).wait_send()
        for block in range(faces):
            face_copy(kind, block).wait_recv()
        got = jnp.concatenate([face_in[kind, block] for block in range(faces)], axis=1)
        return jnp.where(live, got, 0.0)

    def add_faces(value, incoming):
        return jnp.concatenate([value[:, :shared] + incoming, value[:, shared:]], axis=1)

    def product(value, mat_hi, mat_lo, start, stop):
        high, low = halves(value)
        first_part = dot(jnp.concatenate([high, low], axis=0), mat_hi[:, start:stop])
        return first_part[:cases] + first_part[cases:] + dot(high, mat_lo[:, start:stop])

    def push(kind, turn, others, src_of, dst, here, send, recv):
        return [
            remote(src_of(at), dst.at[turn, here], send.at[kind, turn, step], recv.at[kind, turn, here], peer)
            for step, (peer, at) in enumerate(others)
        ]

    def pull(kind, turn, others, src_of, dst, send, recv):
        return [
            remote(src_of(at), dst.at[turn, at], send.at[kind, turn, step], recv.at[kind, turn, at], peer)
            for step, (peer, at) in enumerate(others)
        ]

    def start_all(*args):
        for copy in push(*args):
            copy.start()

    def wait_all(kind, turn, others, src_of, dst, send, recv):
        for copy in pull(kind, turn, others, src_of, dst, send, recv):
            copy.wait_send()
        for copy in pull(kind, turn, others, src_of, dst, send, recv):
            copy.wait_recv()

    def start_gather(turn, field):
        high, low = halves(weight * field)
        out = dot_nt(basis[:32, :], jnp.concatenate([high, low], axis=0))
        value = out[:16] + flip(out[:16]) + out[16:]
        own = jnp.where(left_half, value[:8], flip(value[8:]))
        gather_own[...] = own
        gather[turn, row, spot] = own
        for step, (peer, at) in enumerate(line_others):
            remote(
                gather_own, gather.at[turn, row, spot], line_send.at[0, turn, step], line_recv.at[0, turn, spot], peer
            ).start()

    def pass_gather(turn):
        for receive in (False, True):
            for step, (peer, at) in enumerate(line_others):
                copy = remote(
                    gather_own, gather.at[turn, row, at], line_send.at[0, turn, step], line_recv.at[0, turn, at], peer
                )
                if receive:
                    copy.wait_recv()
                else:
                    copy.wait_send()
        start_all(0, turn, rows_others, lambda at: gather.at[turn, row], gather, row, rows_send, rows_recv)

    def start_spread(turn):
        wait_all(0, turn, rows_others, lambda at: gather.at[turn, row], gather, rows_send, rows_recv)
        packed = gather[turn].reshape(plane, 8, wide)
        turned = flip(packed)
        both = jnp.concatenate(
            [jnp.where(left_half, packed, turned), jnp.where(left_half, turned, packed)], axis=1
        ).reshape(plane * 16, wide)
        high = both.astype(BF16).astype(F32)
        right = jnp.where(left_half, high, both - high).astype(BF16)
        out = dot(coarse_cat[...], right)
        lines = planes * 16
        value = out[:lines] + flip(out[:lines]) + out[lines:]
        value = value.reshape(planes, 2, 8, wide)
        spread_out[...] = jnp.where(left_half, value[:, 0], flip(value[:, 1]))
        spread[turn, deep] = spread_out[deep]
        start_all(0, turn, deep_others, lambda at: spread_out.at[at], spread, deep, deep_send, deep_recv)

    def wait_spread(turn):
        wait_all(0, turn, deep_others, lambda at: spread_out.at[at], spread, deep_send, deep_recv)
        return jnp.sum(spread[turn], axis=0)

    def coarse_field(packed):
        both = jnp.concatenate([packed, flip(packed)], axis=0)
        high = both.astype(BF16).astype(F32)
        stacked = jnp.concatenate([high, high, both - high, jnp.zeros_like(high)], axis=0)
        return dot(stacked.T[:cases].astype(BF16), basis[32:, :])

    def row_sum(value):
        part = value[:, :128]
        for block in range(128, ndof, 128):
            part = part + value[:, block:block + 128]
        part = jnp.sum(part.T, axis=0, keepdims=True)
        return jnp.concatenate([part, part], axis=1)

    def as_column(scalar_row):
        return jnp.broadcast_to(scalar_row, (8, wide)).T[:cases, :1]

    def start_sums(turn, parts):
        own = jnp.concatenate(parts, axis=1)
        sums_own[...] = own
        sums[turn, spot] = own
        start_all(1, turn, line_others, lambda at: sums_own, sums, spot, line_send, line_recv)

    def pass_sums(turn):
        wait_all(1, turn, line_others, lambda at: sums_own, sums, line_send, line_recv)
        own = jnp.sum(sums[turn], axis=0)
        mids_own[...] = own
        mids[turn, row] = own
        start_all(1, turn, rows_others, lambda at: mids_own, mids, row, rows_send, rows_recv)

    def lift_sums(turn):
        wait_all(1, turn, rows_others, lambda at: mids_own, mids, rows_send, rows_recv)
        own = jnp.sum(mids[turn], axis=0)
        tops_own[...] = own
        tops[turn, deep] = own
        start_all(1, turn, deep_others, lambda at: tops_own, tops, deep, deep_send, deep_recv)

    def wait_sums(turn):
        wait_all(1, turn, deep_others, lambda at: tops_own, tops, deep_send, deep_recv)
        total = jnp.sum(tops[turn], axis=0)
        return total[:, :wide], total[:, wide:2 * wide], total[:, 2 * wide:]

    start_faces(1, loads_ref[...])
    for step, (peer, at) in enumerate(deep_others):
        remote(
            coarse_hbm.at[:, coarse_cols(at)], coarse_raw.at[deep], deep_send.at[2, 0, step], deep_recv.at[2, 0, deep], peer
        ).start()
    sol_ref[...] = jnp.zeros_like(sol_ref)
    direction_ref[...] = jnp.zeros_like(direction_ref)
    image_ref[...] = jnp.zeros_like(image_ref)
    scalars[...] = jnp.ones_like(scalars)
    resid = add_faces(loads_ref[...], wait_faces(1))
    start_gather(0, resid)
    res_ref[...] = resid
    load_coarse.wait()
    for receive in (False, True):
        for step, (peer, at) in enumerate(deep_others):
            copy = remote(
                coarse_hbm.at[:, coarse_cols(at)], coarse_raw.at[at], deep_send.at[2, 0, step], deep_recv.at[2, 0, at], peer
            )
            if receive:
                copy.wait_recv()
            else:
                copy.wait_send()
    coarse_hi, coarse_lo = halves(coarse_raw[...].reshape(planes * 16, plane * 16))
    coarse_cat[...] = jnp.concatenate([coarse_hi, coarse_lo], axis=0)
    pass_gather(0)
    local_ref[...] = product(weight * resid, neum_hi, neum_lo, 0, ndof)
    start_spread(0)
    coarse_state[0] = wait_spread(0)
    coarse_state[1] = jnp.zeros_like(coarse_state[1])

    def iterate(step, last):
        now, later = lax.rem(step, 2), lax.rem(step + 1, 2)
        half_sol = weight * (local_ref[...] + coarse_field(coarse_state[0]))
        start_faces(0, half_sol)
        rz_part = row_sum(half_sol * res_ref[...])
        precond = add_faces(half_sol, wait_faces(0))
        near = product(precond, stiff_hi, stiff_lo, 0, shared)
        start_faces(1, near)
        image = jnp.concatenate([near, product(precond, stiff_hi, stiff_lo, shared, ndof)], axis=1)
        zz_part = row_sum(precond * image)
        zq_part = row_sum(weight * precond * image_ref[...])
        start_sums(now, [rz_part, zz_part, zq_part])
        image = add_faces(image, wait_faces(1))
        if not last:
            start_gather(later, image)
        pass_sums(now)
        if not last:
            pass_gather(later)
        lift_sums(now)
        if not last:
            start_spread(later)
        rz, zz, zq = wait_sums(now)
        beta = jnp.where(step > 0, rz / scalars[0:1], 0.0)
        denom = zz + beta * (2.0 * zq) + beta * (beta * jnp.where(step > 0, scalars[1:2], 0.0))
        alpha = rz / denom
        slope, length = as_column(beta), as_column(alpha)
        direction = precond + slope * direction_ref[...]
        image = image + slope * image_ref[...]
        resid = res_ref[...] - length * image
        sol_ref[...] = sol_ref[...] + length * direction
        res_ref[...] = resid
        if not last:
            direction_ref[...] = direction
            image_ref[...] = image
            scalars[0:1] = rz
            scalars[1:2] = denom
            local_ref[...] = product(weight * resid, neum_hi, neum_lo, 0, ndof)
            coarse_image = wait_spread(later) + beta * coarse_state[1]
            coarse_state[1] = coarse_image
            coarse_state[0] = coarse_state[0] - alpha * coarse_image

    def body(step, carry):
        iterate(step, False)
        return carry

    lax.fori_loop(0, ITERS - 1, body, 0)
    iterate(jnp.int32(ITERS - 1), True)


def local(sizes, cycle, stiffness, neumann_inv, coarse_basis, coarse_inv, loads, face_index, face_len):
    cases, ndof = loads.shape[1:]
    faces, width = face_index.shape[1:]
    planes, rows, line = sizes
    plane = rows * line
    wide = 2 * cases
    anywhere = pl.BlockSpec(memory_space=pl.ANY)
    inside = pl.BlockSpec(memory_space=pltpu.VMEM)
    square = jax.ShapeDtypeStruct((ndof, ndof), BF16)
    plain = jax.ShapeDtypeStruct((cases, ndof), F32)
    whole = jax.ShapeDtypeStruct((1, cases, ndof), F32)
    roomy = 56 * 1024 * 1024

    perm, neum_hi, neum_lo, stiff_hi, stiff_lo, basis, fields = pl.pallas_call(
        arrange,
        out_shape=(square,) * 5 + (jax.ShapeDtypeStruct((96, ndof), BF16), plain),
        in_specs=[inside] * 5,
        out_specs=(inside,) * 7,
        scratch_shapes=[pltpu.VMEM((ndof, ndof), BF16)] * 2,
        compiler_params=pltpu.CompilerParams(vmem_limit_bytes=roomy),
        name="arrange",
    )(stiffness, neumann_inv, coarse_basis, loads, face_index)

    sol, res = pl.pallas_call(
        functools.partial(kernel, sizes, cycle),
        out_shape=(plain, plain),
        in_specs=[inside] * 6 + [anywhere, pl.BlockSpec(memory_space=pltpu.SMEM)],
        out_specs=(inside, inside),
        scratch_shapes=[
            pltpu.VMEM((planes, 16, plane * 16), F32),
            pltpu.VMEM((2 * planes * 16, plane * 16), BF16),
            pltpu.VMEM((cases, ndof), F32),
            pltpu.VMEM((cases, ndof), F32),
            pltpu.VMEM((cases, ndof), F32),
            pltpu.VMEM((8, wide), F32),
            pltpu.VMEM((2, 8, wide), F32),
            pltpu.VMEM((2, faces, cases, width), F32),
            pltpu.VMEM((2, faces, cases, width), F32),
            pltpu.VMEM((2, rows, line, 8, wide), F32),
            pltpu.VMEM((8, wide), F32),
            pltpu.VMEM((2, planes, 8, wide), F32),
            pltpu.VMEM((planes, 8, wide), F32),
            pltpu.VMEM((2, line, 1, 3 * wide), F32),
            pltpu.VMEM((1, 3 * wide), F32),
            pltpu.VMEM((2, rows, 1, 3 * wide), F32),
            pltpu.VMEM((1, 3 * wide), F32),
            pltpu.VMEM((2, planes, 1, 3 * wide), F32),
            pltpu.VMEM((1, 3 * wide), F32),
            pltpu.SemaphoreType.DMA,
            pltpu.SemaphoreType.DMA((2, faces)),
            pltpu.SemaphoreType.DMA((2, faces)),
            pltpu.SemaphoreType.DMA((2, 2, line)),
            pltpu.SemaphoreType.DMA((2, 2, line)),
            pltpu.SemaphoreType.DMA((2, 2, rows)),
            pltpu.SemaphoreType.DMA((2, 2, rows)),
            pltpu.SemaphoreType.DMA((3, 2, planes)),
            pltpu.SemaphoreType.DMA((3, 2, planes)),
        ],
        compiler_params=pltpu.CompilerParams(collective_id=0, has_side_effects=True, vmem_limit_bytes=roomy),
        name="solve",
    )(neum_hi, neum_lo, stiff_hi, stiff_lo, basis, fields, coarse_inv, face_len)

    return pl.pallas_call(
        restore,
        out_shape=(whole, whole),
        in_specs=[inside] * 3,
        out_specs=(inside, inside),
        compiler_params=pltpu.CompilerParams(vmem_limit_bytes=roomy),
        name="restore",
    )(sol, res, perm)


def solution(mesh, line=LINE, rows=ROWS, cycle=CYCLE):
    subs = mesh.shape["sub"]
    placed = (
        P("sub", None, None),
        P("sub", None, None),
        P("sub", None, None),
        P("sub", None),
        P("sub", None, None),
        P("sub", None, None),
        P("sub", None),
    )
    return jax.shard_map(
        functools.partial(local, (subs // (rows * line), rows, line), cycle),
        mesh=mesh,
        in_specs=placed,
        out_specs=(P("sub", None, None), P("sub", None, None)),
        check_vma=False,
    )
```

```python
import functools

import jax
import jax.numpy as jnp
from jax import lax
from jax.experimental import pallas as pl
from jax.experimental.pallas import tpu as pltpu
from jax.sharding import PartitionSpec as P

CYCLE = 16
ITERS = 4
LINE = 8
ROWS = 4
MESH = pl.DeviceIdType.MESH
F32 = jnp.float32
BF16 = jnp.bfloat16


def halves(value):
    high = value.astype(BF16)
    return high, (value - high.astype(F32)).astype(BF16)


def thirds(value):
    high = value.astype(BF16)
    rest = value - high.astype(F32)
    mid = rest.astype(BF16)
    return high, mid, (rest - mid.astype(F32)).astype(BF16)


def dot(left, right):
    return jnp.dot(left, right, preferred_element_type=F32)


def dot_nt(left, right):
    return lax.dot_general(left, right, (((1,), (1,)), ((), ())), preferred_element_type=F32)


def iota(shape, dim):
    return lax.broadcasted_iota(jnp.int32, shape, dim)


def three(parts, cases):
    return parts[:cases] + parts[cases:2 * cases] + parts[2 * cases:]


def kernel(
    sizes, cycle, stiff_hbm, neum_hbm, basis_ref, coarse_hbm, loads_ref, index_ref, len_ref, sol_out, res_out,
    raw, perm, turned_hi, turned_lo, neum_hi, neum_lo, stiff_hi, stiff_lo, basis, sol_ref, res_ref,
    coarse_raw, coarse_cat, image_ref, direction_ref, local_ref, scalars, coarse_state, face_out, face_in,
    gather, gather_own, spread, spread_out, sums, sums_own, mids, mids_own, tops, tops_own,
    load_sem, face_send, face_recv, line_send, line_recv, rows_send, rows_recv, deep_send, deep_recv,
):
    planes, rows, line = sizes
    subs, plane = planes * rows * line, rows * line
    cases, ndof = loads_ref.shape[1:]
    faces, width = face_in.shape[1], face_in.shape[3]
    shared = faces * width
    wide = 2 * cases
    me = lax.axis_index("sub")
    deep, col = me // plane, lax.rem(me, plane)
    row, spot = col // line, lax.rem(col, line)
    left_half = iota((1, wide), 1) < cases

    def flip(value):
        return pltpu.roll(value, cases, axis=value.ndim - 1)

    sides = (
        lax.rem(me + subs - 1, subs), lax.rem(me + 1, subs),
        lax.rem(me + subs - cycle, subs), lax.rem(me + cycle, subs),
    )
    line_others = [(me - spot + at, at) for at in [lax.rem(spot + step, line) for step in range(1, line)]]
    rows_others = [(me + (at - row) * line, at) for at in [lax.rem(row + step, rows) for step in range(1, rows)]]
    deep_others = [(me + (at - deep) * plane, at) for at in [lax.rem(deep + step, planes) for step in range(1, planes)]]

    def remote(src, dst, send, recv, peer):
        return pltpu.make_async_remote_copy(
            src_ref=src, dst_ref=dst, send_sem=send, recv_sem=recv, device_id=(peer,), device_id_type=MESH
        )

    def coarse_cols(at):
        return pl.ds(pl.multiple_of(at * (plane * 16), plane * 16), plane * 16)

    load_coarse = pltpu.make_async_copy(coarse_hbm.at[:, coarse_cols(deep)], coarse_raw.at[deep], load_sem.at[2])
    load_neum = pltpu.make_async_copy(neum_hbm.at[0], raw.at[0], load_sem.at[0])
    load_stiff = pltpu.make_async_copy(stiff_hbm.at[0], raw.at[1], load_sem.at[1])
    load_neum.start()
    load_coarse.start()
    load_stiff.start()

    barrier = pltpu.get_barrier_semaphore()
    everyone = [peer for peer, _ in line_others + rows_others + deep_others] + list(sides)
    for peer in everyone:
        pl.semaphore_signal(barrier, inc=1, device_id=(peer,), device_id_type=MESH)
    live = jnp.concatenate([iota((1, width), 1) < len_ref[0, block] for block in range(faces)], axis=1)
    weight = jnp.concatenate([jnp.where(live, 0.5, 1.0), jnp.ones((1, ndof - shared), F32)], axis=1)

    columns = jnp.concatenate([index_ref[0].astype(F32), jnp.zeros((8 - faces, width), F32)], axis=0).T
    for block in range(faces):
        hit = columns[:, block:block + 1].astype(jnp.int32) == iota((width, ndof), 1)
        perm[block * width:(block + 1) * width, :] = jnp.where(hit, 1.0, 0.0).astype(BF16)
    loads_cat = jnp.concatenate(thirds(loads_ref[0]), axis=0)
    first = three(dot_nt(loads_cat, perm[:shared, :]), cases)
    pl.semaphore_wait(barrier, len(everyone))

    def face_copy(kind, block):
        pair = block ^ 1
        return remote(
            face_out.at[kind, block], face_in.at[kind, pair], face_send.at[kind, block], face_recv.at[kind, pair],
            sides[block],
        )

    def start_faces(kind, value):
        for block in range(faces):
            face_out[kind, block] = value[:, block * width:(block + 1) * width]
        for block in range(faces):
            face_copy(kind, block).start()

    def wait_faces(kind):
        for block in range(faces):
            face_copy(kind, block).wait_send()
        for block in range(faces):
            face_copy(kind, block).wait_recv()
        got = jnp.concatenate([face_in[kind, block] for block in range(faces)], axis=1)
        return jnp.where(live, got, 0.0)

    def add_faces(value, incoming):
        return jnp.concatenate([value[:, :shared] + incoming, value[:, shared:]], axis=1)

    def product(value, mat_hi, mat_lo, start, stop):
        high, low = halves(value)
        first_part = dot(jnp.concatenate([high, low], axis=0), mat_hi[:, start:stop])
        return first_part[:cases] + first_part[cases:] + dot(high, mat_lo[:, start:stop])

    def push(kind, turn, others, src_of, dst, here, send, recv):
        return [
            remote(src_of(at), dst.at[turn, here], send.at[kind, turn, step], recv.at[kind, turn, here], peer)
            for step, (peer, at) in enumerate(others)
        ]

    def pull(kind, turn, others, src_of, dst, send, recv):
        return [
            remote(src_of(at), dst.at[turn, at], send.at[kind, turn, step], recv.at[kind, turn, at], peer)
            for step, (peer, at) in enumerate(others)
        ]

    def start_all(*args):
        for copy in push(*args):
            copy.start()

    def wait_all(kind, turn, others, src_of, dst, send, recv):
        for copy in pull(kind, turn, others, src_of, dst, send, recv):
            copy.wait_send()
        for copy in pull(kind, turn, others, src_of, dst, send, recv):
            copy.wait_recv()

    def start_gather(turn, field):
        high, low = halves(weight * field)
        out = dot_nt(basis[:32, :], jnp.concatenate([high, low], axis=0))
        value = out[:16] + flip(out[:16]) + out[16:]
        own = jnp.where(left_half, value[:8], flip(value[8:]))
        gather_own[...] = own
        gather[turn, row, spot] = own
        for step, (peer, at) in enumerate(line_others):
            remote(
                gather_own, gather.at[turn, row, spot], line_send.at[0, turn, step], line_recv.at[0, turn, spot], peer
            ).start()

    def pass_gather(turn):
        for receive in (False, True):
            for step, (peer, at) in enumerate(line_others):
                copy = remote(
                    gather_own, gather.at[turn, row, at], line_send.at[0, turn, step], line_recv.at[0, turn, at], peer
                )
                if receive:
                    copy.wait_recv()
                else:
                    copy.wait_send()
        start_all(0, turn, rows_others, lambda at: gather.at[turn, row], gather, row, rows_send, rows_recv)

    def start_spread(turn):
        wait_all(0, turn, rows_others, lambda at: gather.at[turn, row], gather, rows_send, rows_recv)
        packed = gather[turn].reshape(plane, 8, wide)
        turned = flip(packed)
        both = jnp.concatenate(
            [jnp.where(left_half, packed, turned), jnp.where(left_half, turned, packed)], axis=1
        ).reshape(plane * 16, wide)
        high = both.astype(BF16).astype(F32)
        right = jnp.where(left_half, high, both - high).astype(BF16)
        out = dot(coarse_cat[...], right)
        lines = planes * 16
        value = out[:lines] + flip(out[:lines]) + out[lines:]
        value = value.reshape(planes, 2, 8, wide)
        spread_out[...] = jnp.where(left_half, value[:, 0], flip(value[:, 1]))
        spread[turn, deep] = spread_out[deep]
        start_all(0, turn, deep_others, lambda at: spread_out.at[at], spread, deep, deep_send, deep_recv)

    def wait_spread(turn):
        wait_all(0, turn, deep_others, lambda at: spread_out.at[at], spread, deep_send, deep_recv)
        return jnp.sum(spread[turn], axis=0)

    def coarse_field(packed):
        both = jnp.concatenate([packed, flip(packed)], axis=0)
        high = both.astype(BF16).astype(F32)
        stacked = jnp.concatenate([high, high, both - high, jnp.zeros_like(high)], axis=0)
        return dot(stacked.T[:cases].astype(BF16), basis[32:, :])

    def row_sum(value):
        part = value[:, :128]
        for block in range(128, ndof, 128):
            part = part + value[:, block:block + 128]
        part = jnp.sum(part.T, axis=0, keepdims=True)
        return jnp.concatenate([part, part], axis=1)

    def as_column(scalar_row):
        return jnp.broadcast_to(scalar_row, (8, wide)).T[:cases, :1]

    def start_sums(turn, parts):
        own = jnp.concatenate(parts, axis=1)
        sums_own[...] = own
        sums[turn, spot] = own
        start_all(1, turn, line_others, lambda at: sums_own, sums, spot, line_send, line_recv)

    def pass_sums(turn):
        wait_all(1, turn, line_others, lambda at: sums_own, sums, line_send, line_recv)
        own = jnp.sum(sums[turn], axis=0)
        mids_own[...] = own
        mids[turn, row] = own
        start_all(1, turn, rows_others, lambda at: mids_own, mids, row, rows_send, rows_recv)

    def lift_sums(turn):
        wait_all(1, turn, rows_others, lambda at: mids_own, mids, rows_send, rows_recv)
        own = jnp.sum(mids[turn], axis=0)
        tops_own[...] = own
        tops[turn, deep] = own
        start_all(1, turn, deep_others, lambda at: tops_own, tops, deep, deep_send, deep_recv)

    def wait_sums(turn):
        wait_all(1, turn, deep_others, lambda at: tops_own, tops, deep_send, deep_recv)
        total = jnp.sum(tops[turn], axis=0)
        return total[:, :wide], total[:, wide:2 * wide], total[:, 2 * wide:]

    tall = 256

    def turn(which, start, stop):
        def block(step, carry):
            here = pl.ds(pl.multiple_of(step * tall, tall), tall)
            high, low = halves(raw[which, here, :])
            both = dot_nt(jnp.concatenate([high, low], axis=0), perm[start:stop, :]).astype(BF16)
            turned_hi[here, start:stop] = both[:tall]
            turned_lo[here, start:stop] = both[tall:]
            return carry

        lax.fori_loop(0, ndof // tall, block, 0)

    def settle(out_hi, out_lo, start, stop, begin, end):
        def block(step, carry):
            here = pl.ds(pl.multiple_of(step * tall, tall), tall)
            pick = perm[here, :]
            out_hi[here, start:stop] = dot(pick, turned_hi[:, start:stop]).astype(BF16)
            out_lo[here, start:stop] = dot(pick, turned_lo[:, start:stop]).astype(BF16)
            return carry

        lax.fori_loop(begin, end, block, 0)

    start_faces(1, first)
    for step, (peer, at) in enumerate(deep_others):
        remote(
            coarse_hbm.at[:, coarse_cols(at)], coarse_raw.at[deep], deep_send.at[2, 0, step], deep_recv.at[2, 0, deep], peer
        ).start()
    sol_ref[...] = jnp.zeros_like(sol_ref)
    direction_ref[...] = jnp.zeros_like(direction_ref)
    image_ref[...] = jnp.zeros_like(image_ref)
    scalars[...] = jnp.ones_like(scalars)

    taken = dot(jnp.ones((16, shared), BF16), perm[:shared, :])[:8]
    free = (1.0 - taken).astype(BF16)
    rank = jnp.zeros((8, ndof), F32)
    for block in range(0, ndof, 128):
        before = jnp.where(iota((128, ndof), 0) + block < iota((128, ndof), 1), 1.0, 0.0).astype(BF16)
        rank = rank + dot(free[:, block:block + 128], before)
    place = jnp.where(taken[:1] > 0.5, -1.0, rank[:1]).astype(jnp.int32)
    for block in range(0, ndof - shared, 128):
        hit = place == iota((128, ndof), 0) + block
        perm[shared + block:shared + block + 128, :] = jnp.where(hit, 1.0, 0.0).astype(BF16)
    rest = three(dot_nt(loads_cat, perm[shared:, :]), cases)
    basis_hi, basis_lo = halves(three(dot_nt(jnp.concatenate(thirds(basis_ref[0]), axis=0), perm[...]), 16))
    basis[...] = jnp.concatenate(
        [basis_hi, basis_lo, basis_hi, basis_lo, basis_hi, jnp.zeros_like(basis_hi)], axis=0
    )
    load_neum.wait()
    turn(0, 0, ndof)
    resid = jnp.concatenate([first + wait_faces(1), rest], axis=1)
    start_gather(0, resid)
    res_ref[...] = resid
    load_coarse.wait()
    for receive in (False, True):
        for step, (peer, at) in enumerate(deep_others):
            copy = remote(
                coarse_hbm.at[:, coarse_cols(at)], coarse_raw.at[at], deep_send.at[2, 0, step], deep_recv.at[2, 0, at], peer
            )
            if receive:
                copy.wait_recv()
            else:
                copy.wait_send()
    coarse_hi, coarse_lo = halves(coarse_raw[...].reshape(planes * 16, plane * 16))
    coarse_cat[...] = jnp.concatenate([coarse_hi, coarse_lo], axis=0)
    half_way = ndof // tall // 2
    settle(neum_hi, neum_lo, 0, ndof, 0, half_way)
    pass_gather(0)
    settle(neum_hi, neum_lo, 0, ndof, half_way, 2 * half_way)
    start_spread(0)
    local_ref[...] = product(weight * res_ref[...], neum_hi, neum_lo, 0, ndof)
    load_stiff.wait()
    turn(1, 0, shared)
    coarse_state[0] = wait_spread(0)
    coarse_state[1] = jnp.zeros_like(coarse_state[1])

    def iterate(step, last):
        now, later = (step % 2, (step + 1) % 2) if last else (lax.rem(step, 2), lax.rem(step + 1, 2))
        half_sol = weight * (local_ref[...] + coarse_field(coarse_state[0]))
        start_faces(0, half_sol)
        rz_part = row_sum(half_sol * res_ref[...])

        if not last:
            @pl.when(step == 0)
            def _():
                settle(stiff_hi, stiff_lo, 0, shared, 0, ndof // tall)

        precond = add_faces(half_sol, wait_faces(0))
        near = product(precond, stiff_hi, stiff_lo, 0, shared)
        start_faces(1, near)

        if not last:
            @pl.when(step == 0)
            def _():
                turn(1, shared, ndof)
                settle(stiff_hi, stiff_lo, shared, ndof, 0, ndof // tall)

        image = jnp.concatenate([near, product(precond, stiff_hi, stiff_lo, shared, ndof)], axis=1)
        zz_part = row_sum(precond * image)
        zq_part = row_sum(weight * precond * image_ref[...])
        start_sums(now, [rz_part, zz_part, zq_part])
        image = add_faces(image, wait_faces(1))
        if not last:
            start_gather(later, image)
        pass_sums(now)
        if not last:
            pass_gather(later)
        lift_sums(now)
        if not last:
            start_spread(later)
        rz, zz, zq = wait_sums(now)
        beta = jnp.where(step > 0, rz / scalars[0:1], 0.0)
        denom = zz + beta * (2.0 * zq) + beta * (beta * jnp.where(step > 0, scalars[1:2], 0.0))
        alpha = rz / denom
        slope, length = as_column(beta), as_column(alpha)
        direction = precond + slope * direction_ref[...]
        image = image + slope * image_ref[...]
        resid = res_ref[...] - length * image
        sol_ref[...] = sol_ref[...] + length * direction
        res_ref[...] = resid
        if not last:
            direction_ref[...] = direction
            image_ref[...] = image
            scalars[0:1] = rz
            scalars[1:2] = denom
            local_ref[...] = product(weight * resid, neum_hi, neum_lo, 0, ndof)
            coarse_image = wait_spread(later) + beta * coarse_state[1]
            coarse_state[1] = coarse_image
            coarse_state[0] = coarse_state[0] - alpha * coarse_image

    def body(step, carry):
        iterate(step, False)
        return carry

    lax.fori_loop(0, ITERS - 1, body, 0)
    iterate(ITERS - 1, True)
    sol_out[0] = three(dot(jnp.concatenate(thirds(sol_ref[...]), axis=0), perm[...]), cases)
    res_out[0] = three(dot(jnp.concatenate(thirds(res_ref[...]), axis=0), perm[...]), cases)


def local(sizes, cycle, stiffness, neumann_inv, coarse_basis, coarse_inv, loads, face_index, face_len):
    cases, ndof = loads.shape[1:]
    faces, width = face_index.shape[1:]
    planes, rows, line = sizes
    plane = rows * line
    wide = 2 * cases
    anywhere = pl.BlockSpec(memory_space=pl.ANY)
    inside = pl.BlockSpec(memory_space=pltpu.VMEM)
    square = pltpu.VMEM((ndof, ndof), BF16)
    plain = pltpu.VMEM((cases, ndof), F32)
    whole = jax.ShapeDtypeStruct((1, cases, ndof), F32)
    return pl.pallas_call(
        functools.partial(kernel, sizes, cycle),
        out_shape=(whole, whole),
        in_specs=[anywhere, anywhere, inside, anywhere, inside, inside, pl.BlockSpec(memory_space=pltpu.SMEM)],
        out_specs=(inside, inside),
        scratch_shapes=[
            pltpu.VMEM((2, ndof, ndof), F32),
            square, square, square, square, square, square, square,
            pltpu.VMEM((96, ndof), BF16),
            plain, plain,
            pltpu.VMEM((planes, 16, plane * 16), F32),
            pltpu.VMEM((2 * planes * 16, plane * 16), BF16),
            pltpu.VMEM((cases, ndof), F32),
            pltpu.VMEM((cases, ndof), F32),
            pltpu.VMEM((cases, ndof), F32),
            pltpu.VMEM((8, wide), F32),
            pltpu.VMEM((2, 8, wide), F32),
            pltpu.VMEM((2, faces, cases, width), F32),
            pltpu.VMEM((2, faces, cases, width), F32),
            pltpu.VMEM((2, rows, line, 8, wide), F32),
            pltpu.VMEM((8, wide), F32),
            pltpu.VMEM((2, planes, 8, wide), F32),
            pltpu.VMEM((planes, 8, wide), F32),
            pltpu.VMEM((2, line, 1, 3 * wide), F32),
            pltpu.VMEM((1, 3 * wide), F32),
            pltpu.VMEM((2, rows, 1, 3 * wide), F32),
            pltpu.VMEM((1, 3 * wide), F32),
            pltpu.VMEM((2, planes, 1, 3 * wide), F32),
            pltpu.VMEM((1, 3 * wide), F32),
            pltpu.SemaphoreType.DMA((3,)),
            pltpu.SemaphoreType.DMA((2, faces)),
            pltpu.SemaphoreType.DMA((2, faces)),
            pltpu.SemaphoreType.DMA((2, 2, line)),
            pltpu.SemaphoreType.DMA((2, 2, line)),
            pltpu.SemaphoreType.DMA((2, 2, rows)),
            pltpu.SemaphoreType.DMA((2, 2, rows)),
            pltpu.SemaphoreType.DMA((3, 2, planes)),
            pltpu.SemaphoreType.DMA((3, 2, planes)),
        ],
        compiler_params=pltpu.CompilerParams(
            collective_id=0, has_side_effects=True, vmem_limit_bytes=56 * 1024 * 1024
        ),
        name="solve",
    )(stiffness, neumann_inv, coarse_basis, coarse_inv, loads, face_index, face_len)


def solution(mesh, line=LINE, rows=ROWS, cycle=CYCLE):
    subs = mesh.shape["sub"]
    placed = (
        P("sub", None, None),
        P("sub", None, None),
        P("sub", None, None),
        P("sub", None),
        P("sub", None, None),
        P("sub", None, None),
        P("sub", None),
    )
    return jax.shard_map(
        functools.partial(local, (subs // (rows * line), rows, line), cycle),
        mesh=mesh,
        in_specs=placed,
        out_specs=(P("sub", None, None), P("sub", None, None)),
        check_vma=False,
    )
```

```python
import functools

import jax
import jax.numpy as jnp
from jax import lax
from jax.experimental import pallas as pl
from jax.experimental.pallas import tpu as pltpu
from jax.sharding import PartitionSpec as P

CYCLE = 16
ITERS = 4
PLANE = 32
MESH = pl.DeviceIdType.MESH
F32 = jnp.float32
BF16 = jnp.bfloat16


def halves(value):
    high = value.astype(BF16)
    return high, (value - high.astype(F32)).astype(BF16)


def thirds(value):
    high = value.astype(BF16)
    rest = value - high.astype(F32)
    mid = rest.astype(BF16)
    return high, mid, (rest - mid.astype(F32)).astype(BF16)


def dot(left, right):
    return jnp.dot(left, right, preferred_element_type=F32)


def dot_nt(left, right):
    return lax.dot_general(left, right, (((1,), (1,)), ((), ())), preferred_element_type=F32)


def iota(shape, dim):
    return lax.broadcasted_iota(jnp.int32, shape, dim)


def three(parts, cases):
    return parts[:cases] + parts[cases:2 * cases] + parts[2 * cases:]


def kernel(
    sizes, cycle, stiff_hbm, neum_hbm, basis_ref, coarse_hbm, loads_ref, index_ref, len_ref, sol_out, res_out,
    raw, perm, turned_hi, turned_lo, neum_hi, neum_lo, stiff_hi, stiff_lo, basis, sol_ref, res_ref,
    coarse_raw, coarse_cat, image_ref, direction_ref, local_ref, scalars, coarse_state, face_out, face_in,
    gather, gather_own, spread, spread_out, sums, sums_own, tops, tops_own,
    load_sem, face_send, face_recv, flat_send, flat_recv, deep_send, deep_recv,
):
    planes, plane = sizes
    subs = planes * plane
    cases, ndof = loads_ref.shape[1:]
    faces, width = face_in.shape[1], face_in.shape[3]
    shared = faces * width
    wide = 2 * cases
    me = lax.axis_index("sub")
    deep, col = me // plane, lax.rem(me, plane)
    left_half = iota((1, wide), 1) < cases

    def flip(value):
        return pltpu.roll(value, cases, axis=value.ndim - 1)

    sides = (
        lax.rem(me + subs - 1, subs), lax.rem(me + 1, subs),
        lax.rem(me + subs - cycle, subs), lax.rem(me + cycle, subs),
    )
    flat_others = [(me - col + at, at) for at in [lax.rem(col + step, plane) for step in range(1, plane)]]
    deep_others = [(me + (at - deep) * plane, at) for at in [lax.rem(deep + step, planes) for step in range(1, planes)]]

    def remote(src, dst, send, recv, peer):
        return pltpu.make_async_remote_copy(
            src_ref=src, dst_ref=dst, send_sem=send, recv_sem=recv, device_id=(peer,), device_id_type=MESH
        )

    def coarse_cols(at):
        return pl.ds(pl.multiple_of(at * (plane * 16), plane * 16), plane * 16)

    load_coarse = pltpu.make_async_copy(coarse_hbm.at[:, coarse_cols(deep)], coarse_raw.at[deep], load_sem.at[2])
    load_neum = pltpu.make_async_copy(neum_hbm.at[0], raw.at[0], load_sem.at[0])
    load_stiff = pltpu.make_async_copy(stiff_hbm.at[0], raw.at[1], load_sem.at[1])
    load_neum.start()
    load_coarse.start()
    load_stiff.start()

    barrier = pltpu.get_barrier_semaphore()
    everyone = [peer for peer, _ in flat_others + deep_others] + list(sides)
    for peer in everyone:
        pl.semaphore_signal(barrier, inc=1, device_id=(peer,), device_id_type=MESH)
    live = jnp.concatenate([iota((1, width), 1) < len_ref[0, block] for block in range(faces)], axis=1)
    weight = jnp.concatenate([jnp.where(live, 0.5, 1.0), jnp.ones((1, ndof - shared), F32)], axis=1)

    columns = jnp.concatenate([index_ref[0].astype(F32), jnp.zeros((8 - faces, width), F32)], axis=0).T
    for block in range(faces):
        hit = columns[:, block:block + 1].astype(jnp.int32) == iota((width, ndof), 1)
        perm[block * width:(block + 1) * width, :] = jnp.where(hit, 1.0, 0.0).astype(BF16)
    loads_cat = jnp.concatenate(thirds(loads_ref[0]), axis=0)
    first = three(dot_nt(loads_cat, perm[:shared, :]), cases)
    pl.semaphore_wait(barrier, len(everyone))

    def face_copy(kind, block):
        pair = block ^ 1
        return remote(
            face_out.at[kind, block], face_in.at[kind, pair], face_send.at[kind, block], face_recv.at[kind, pair],
            sides[block],
        )

    def start_faces(kind, value):
        for block in range(faces):
            face_out[kind, block] = value[:, block * width:(block + 1) * width]
        for block in range(faces):
            face_copy(kind, block).start()

    def wait_faces(kind):
        for block in range(faces):
            face_copy(kind, block).wait_send()
        for block in range(faces):
            face_copy(kind, block).wait_recv()
        got = jnp.concatenate([face_in[kind, block] for block in range(faces)], axis=1)
        return jnp.where(live, got, 0.0)

    def add_faces(value, incoming):
        return jnp.concatenate([value[:, :shared] + incoming, value[:, shared:]], axis=1)

    def product(value, mat_hi, mat_lo, start, stop):
        high, low = halves(value)
        first_part = dot(jnp.concatenate([high, low], axis=0), mat_hi[:, start:stop])
        return first_part[:cases] + first_part[cases:] + dot(high, mat_lo[:, start:stop])

    def push(kind, turn, others, src_of, dst, here, send, recv):
        return [
            remote(src_of(at), dst.at[turn, here], send.at[kind, turn, step], recv.at[kind, turn, here], peer)
            for step, (peer, at) in enumerate(others)
        ]

    def pull(kind, turn, others, src_of, dst, send, recv):
        return [
            remote(src_of(at), dst.at[turn, at], send.at[kind, turn, step], recv.at[kind, turn, at], peer)
            for step, (peer, at) in enumerate(others)
        ]

    def start_all(*args):
        for copy in push(*args):
            copy.start()

    def wait_all(kind, turn, others, src_of, dst, send, recv):
        for copy in pull(kind, turn, others, src_of, dst, send, recv):
            copy.wait_send()
        for copy in pull(kind, turn, others, src_of, dst, send, recv):
            copy.wait_recv()

    def start_gather(turn, field):
        high, low = halves(weight * field)
        out = dot_nt(basis[:32, :], jnp.concatenate([high, low], axis=0))
        value = out[:16] + flip(out[:16]) + out[16:]
        own = jnp.where(left_half, value[:8], flip(value[8:]))
        gather_own[...] = own
        gather[turn, col] = own
        start_all(0, turn, flat_others, lambda at: gather_own, gather, col, flat_send, flat_recv)

    def start_spread(turn):
        wait_all(0, turn, flat_others, lambda at: gather_own, gather, flat_send, flat_recv)
        packed = gather[turn]
        turned = flip(packed)
        both = jnp.concatenate(
            [jnp.where(left_half, packed, turned), jnp.where(left_half, turned, packed)], axis=1
        ).reshape(plane * 16, wide)
        high = both.astype(BF16).astype(F32)
        right = jnp.where(left_half, high, both - high).astype(BF16)
        out = dot(coarse_cat[...], right)
        lines = planes * 16
        value = out[:lines] + flip(out[:lines]) + out[lines:]
        value = value.reshape(planes, 2, 8, wide)
        spread_out[...] = jnp.where(left_half, value[:, 0], flip(value[:, 1]))
        spread[turn, deep] = spread_out[deep]
        start_all(0, turn, deep_others, lambda at: spread_out.at[at], spread, deep, deep_send, deep_recv)

    def wait_spread(turn):
        wait_all(0, turn, deep_others, lambda at: spread_out.at[at], spread, deep_send, deep_recv)
        return jnp.sum(spread[turn], axis=0)

    def coarse_field(packed):
        both = jnp.concatenate([packed, flip(packed)], axis=0)
        high = both.astype(BF16).astype(F32)
        stacked = jnp.concatenate([high, high, both - high, jnp.zeros_like(high)], axis=0)
        return dot(stacked.T[:cases].astype(BF16), basis[32:, :])

    def row_sum(value):
        part = value[:, :128]
        for block in range(128, ndof, 128):
            part = part + value[:, block:block + 128]
        part = jnp.sum(part.T, axis=0, keepdims=True)
        return jnp.concatenate([part, part], axis=1)

    def as_column(scalar_row):
        return jnp.broadcast_to(scalar_row, (8, wide)).T[:cases, :1]

    def start_sums(turn, parts):
        own = jnp.concatenate(parts, axis=1)
        sums_own[...] = own
        sums[turn, col] = own
        start_all(1, turn, flat_others, lambda at: sums_own, sums, col, flat_send, flat_recv)

    def lift_sums(turn):
        wait_all(1, turn, flat_others, lambda at: sums_own, sums, flat_send, flat_recv)
        own = jnp.sum(sums[turn], axis=0)
        tops_own[...] = own
        tops[turn, deep] = own
        start_all(1, turn, deep_others, lambda at: tops_own, tops, deep, deep_send, deep_recv)

    def wait_sums(turn):
        wait_all(1, turn, deep_others, lambda at: tops_own, tops, deep_send, deep_recv)
        total = jnp.sum(tops[turn], axis=0)
        return total[:, :wide], total[:, wide:2 * wide], total[:, 2 * wide:]

    tall = 256

    def turn(which, start, stop):
        def block(step, carry):
            here = pl.ds(pl.multiple_of(step * tall, tall), tall)
            high, low = halves(raw[which, here, :])
            both = dot_nt(jnp.concatenate([high, low], axis=0), perm[start:stop, :]).astype(BF16)
            turned_hi[here, start:stop] = both[:tall]
            turned_lo[here, start:stop] = both[tall:]
            return carry

        lax.fori_loop(0, ndof // tall, block, 0)

    def settle(out_hi, out_lo, start, stop, begin, end):
        def block(step, carry):
            here = pl.ds(pl.multiple_of(step * tall, tall), tall)
            pick = perm[here, :]
            out_hi[here, start:stop] = dot(pick, turned_hi[:, start:stop]).astype(BF16)
            out_lo[here, start:stop] = dot(pick, turned_lo[:, start:stop]).astype(BF16)
            return carry

        lax.fori_loop(begin, end, block, 0)

    start_faces(1, first)
    for step, (peer, at) in enumerate(deep_others):
        remote(
            coarse_hbm.at[:, coarse_cols(at)], coarse_raw.at[deep], deep_send.at[2, 0, step], deep_recv.at[2, 0, deep], peer
        ).start()
    sol_ref[...] = jnp.zeros_like(sol_ref)
    direction_ref[...] = jnp.zeros_like(direction_ref)
    image_ref[...] = jnp.zeros_like(image_ref)
    scalars[...] = jnp.ones_like(scalars)

    taken = dot(jnp.ones((16, shared), BF16), perm[:shared, :])[:8]
    free = (1.0 - taken).astype(BF16)
    rank = jnp.zeros((8, ndof), F32)
    for block in range(0, ndof, 128):
        before = jnp.where(iota((128, ndof), 0) + block < iota((128, ndof), 1), 1.0, 0.0).astype(BF16)
        rank = rank + dot(free[:, block:block + 128], before)
    place = jnp.where(taken[:1] > 0.5, -1.0, rank[:1]).astype(jnp.int32)
    for block in range(0, ndof - shared, 128):
        hit = place == iota((128, ndof), 0) + block
        perm[shared + block:shared + block + 128, :] = jnp.where(hit, 1.0, 0.0).astype(BF16)
    rest = three(dot_nt(loads_cat, perm[shared:, :]), cases)
    basis_hi, basis_lo = halves(three(dot_nt(jnp.concatenate(thirds(basis_ref[0]), axis=0), perm[...]), 16))
    basis[...] = jnp.concatenate(
        [basis_hi, basis_lo, basis_hi, basis_lo, basis_hi, jnp.zeros_like(basis_hi)], axis=0
    )
    load_neum.wait()
    turn(0, 0, ndof)
    resid = jnp.concatenate([first + wait_faces(1), rest], axis=1)
    start_gather(0, resid)
    res_ref[...] = resid
    load_coarse.wait()
    for receive in (False, True):
        for step, (peer, at) in enumerate(deep_others):
            copy = remote(
                coarse_hbm.at[:, coarse_cols(at)], coarse_raw.at[at], deep_send.at[2, 0, step], deep_recv.at[2, 0, at], peer
            )
            if receive:
                copy.wait_recv()
            else:
                copy.wait_send()
    coarse_hi, coarse_lo = halves(coarse_raw[...].reshape(planes * 16, plane * 16))
    coarse_cat[...] = jnp.concatenate([coarse_hi, coarse_lo], axis=0)
    settle(neum_hi, neum_lo, 0, ndof, 0, ndof // tall)
    start_spread(0)
    local_ref[...] = product(weight * res_ref[...], neum_hi, neum_lo, 0, ndof)
    load_stiff.wait()
    turn(1, 0, shared)
    coarse_state[0] = wait_spread(0)
    coarse_state[1] = jnp.zeros_like(coarse_state[1])

    def iterate(step, last):
        now, later = (step % 2, (step + 1) % 2) if last else (lax.rem(step, 2), lax.rem(step + 1, 2))
        half_sol = weight * (local_ref[...] + coarse_field(coarse_state[0]))
        start_faces(0, half_sol)
        rz_part = row_sum(half_sol * res_ref[...])

        if not last:
            @pl.when(step == 0)
            def _():
                settle(stiff_hi, stiff_lo, 0, shared, 0, ndof // tall)

        precond = add_faces(half_sol, wait_faces(0))
        near = product(precond, stiff_hi, stiff_lo, 0, shared)
        start_faces(1, near)

        if not last:
            @pl.when(step == 0)
            def _():
                turn(1, shared, ndof)
                settle(stiff_hi, stiff_lo, shared, ndof, 0, ndof // tall)

        image = jnp.concatenate([near, product(precond, stiff_hi, stiff_lo, shared, ndof)], axis=1)
        zz_part = row_sum(precond * image)
        zq_part = row_sum(weight * precond * image_ref[...])
        start_sums(now, [rz_part, zz_part, zq_part])
        image = add_faces(image, wait_faces(1))
        if not last:
            start_gather(later, image)
        lift_sums(now)
        if not last:
            start_spread(later)
        rz, zz, zq = wait_sums(now)
        beta = jnp.where(step > 0, rz / scalars[0:1], 0.0)
        denom = zz + beta * (2.0 * zq) + beta * (beta * jnp.where(step > 0, scalars[1:2], 0.0))
        alpha = rz / denom
        slope, length = as_column(beta), as_column(alpha)
        direction = precond + slope * direction_ref[...]
        image = image + slope * image_ref[...]
        resid = res_ref[...] - length * image
        sol_ref[...] = sol_ref[...] + length * direction
        res_ref[...] = resid
        if not last:
            direction_ref[...] = direction
            image_ref[...] = image
            scalars[0:1] = rz
            scalars[1:2] = denom
            local_ref[...] = product(weight * resid, neum_hi, neum_lo, 0, ndof)
            coarse_image = wait_spread(later) + beta * coarse_state[1]
            coarse_state[1] = coarse_image
            coarse_state[0] = coarse_state[0] - alpha * coarse_image

    def body(step, carry):
        iterate(step, False)
        return carry

    lax.fori_loop(0, ITERS - 1, body, 0)
    iterate(ITERS - 1, True)
    sol_out[0] = three(dot(jnp.concatenate(thirds(sol_ref[...]), axis=0), perm[...]), cases)
    res_out[0] = three(dot(jnp.concatenate(thirds(res_ref[...]), axis=0), perm[...]), cases)


def local(sizes, cycle, stiffness, neumann_inv, coarse_basis, coarse_inv, loads, face_index, face_len):
    cases, ndof = loads.shape[1:]
    faces, width = face_index.shape[1:]
    planes, plane = sizes
    wide = 2 * cases
    anywhere = pl.BlockSpec(memory_space=pl.ANY)
    inside = pl.BlockSpec(memory_space=pltpu.VMEM)
    square = pltpu.VMEM((ndof, ndof), BF16)
    plain = pltpu.VMEM((cases, ndof), F32)
    whole = jax.ShapeDtypeStruct((1, cases, ndof), F32)
    return pl.pallas_call(
        functools.partial(kernel, sizes, cycle),
        out_shape=(whole, whole),
        in_specs=[anywhere, anywhere, inside, anywhere, inside, inside, pl.BlockSpec(memory_space=pltpu.SMEM)],
        out_specs=(inside, inside),
        scratch_shapes=[
            pltpu.VMEM((2, ndof, ndof), F32),
            square, square, square, square, square, square, square,
            pltpu.VMEM((96, ndof), BF16),
            plain, plain,
            pltpu.VMEM((planes, 16, plane * 16), F32),
            pltpu.VMEM((2 * planes * 16, plane * 16), BF16),
            pltpu.VMEM((cases, ndof), F32),
            pltpu.VMEM((cases, ndof), F32),
            pltpu.VMEM((cases, ndof), F32),
            pltpu.VMEM((8, wide), F32),
            pltpu.VMEM((2, 8, wide), F32),
            pltpu.VMEM((2, faces, cases, width), F32),
            pltpu.VMEM((2, faces, cases, width), F32),
            pltpu.VMEM((2, plane, 8, wide), F32),
            pltpu.VMEM((8, wide), F32),
            pltpu.VMEM((2, planes, 8, wide), F32),
            pltpu.VMEM((planes, 8, wide), F32),
            pltpu.VMEM((2, plane, 1, 3 * wide), F32),
            pltpu.VMEM((1, 3 * wide), F32),
            pltpu.VMEM((2, planes, 1, 3 * wide), F32),
            pltpu.VMEM((1, 3 * wide), F32),
            pltpu.SemaphoreType.DMA((3,)),
            pltpu.SemaphoreType.DMA((2, faces)),
            pltpu.SemaphoreType.DMA((2, faces)),
            pltpu.SemaphoreType.DMA((2, 2, plane)),
            pltpu.SemaphoreType.DMA((2, 2, plane)),
            pltpu.SemaphoreType.DMA((3, 2, planes)),
            pltpu.SemaphoreType.DMA((3, 2, planes)),
        ],
        compiler_params=pltpu.CompilerParams(
            collective_id=0, has_side_effects=True, vmem_limit_bytes=56 * 1024 * 1024
        ),
        name="solve",
    )(stiffness, neumann_inv, coarse_basis, coarse_inv, loads, face_index, face_len)


def solution(mesh, plane=PLANE, cycle=CYCLE):
    subs = mesh.shape["sub"]
    placed = (
        P("sub", None, None),
        P("sub", None, None),
        P("sub", None, None),
        P("sub", None),
        P("sub", None, None),
        P("sub", None, None),
        P("sub", None),
    )
    return jax.shard_map(
        functools.partial(local, (subs // plane, plane), cycle),
        mesh=mesh,
        in_specs=placed,
        out_specs=(P("sub", None, None), P("sub", None, None)),
        check_vma=False,
    )
```

```python
import functools

import jax
import jax.numpy as jnp
from jax import lax
from jax.experimental import pallas as pl
from jax.experimental.pallas import tpu as pltpu
from jax.sharding import PartitionSpec as P

CYCLE = 16
ITERS = 4
PLANE = 32
MESH = pl.DeviceIdType.MESH
F32 = jnp.float32
BF16 = jnp.bfloat16


def halves(value):
    high = value.astype(BF16)
    return high, (value - high.astype(F32)).astype(BF16)


def thirds(value):
    high = value.astype(BF16)
    rest = value - high.astype(F32)
    mid = rest.astype(BF16)
    return high, mid, (rest - mid.astype(F32)).astype(BF16)


def dot(left, right):
    return jnp.dot(left, right, preferred_element_type=F32)


def dot_nt(left, right):
    return lax.dot_general(left, right, (((1,), (1,)), ((), ())), preferred_element_type=F32)


def iota(shape, dim):
    return lax.broadcasted_iota(jnp.int32, shape, dim)


def three(parts, cases):
    return parts[:cases] + parts[cases:2 * cases] + parts[2 * cases:]


def kernel(
    sizes, cycle, stiff_hbm, neum_hbm, basis_ref, coarse_hbm, loads_ref, index_ref, len_ref, sol_out, res_out,
    raw, perm, turned_hi, turned_lo, neum_hi, neum_lo, stiff_hi, stiff_lo, basis, sol_ref, res_ref,
    coarse_raw, coarse_cat, image_ref, direction_ref, local_ref, scalars, coarse_state, face_out, face_in,
    gather, gather_own, spread, spread_out, sums, sums_own, tops, tops_own,
    load_sem, face_send, face_recv, flat_send, flat_recv, deep_send, deep_recv,
):
    planes, plane = sizes
    subs = planes * plane
    cases, ndof = loads_ref.shape[1:]
    faces, width = face_in.shape[1], face_in.shape[3]
    shared = faces * width
    wide = 2 * cases
    me = lax.axis_index("sub")
    deep, col = me // plane, lax.rem(me, plane)
    left_half = iota((1, wide), 1) < cases

    def flip(value):
        return pltpu.roll(value, cases, axis=value.ndim - 1)

    sides = (
        lax.rem(me + subs - 1, subs), lax.rem(me + 1, subs),
        lax.rem(me + subs - cycle, subs), lax.rem(me + cycle, subs),
    )
    flat_others = [(me - col + at, at) for at in [lax.rem(col + step, plane) for step in range(1, plane)]]
    deep_others = [(me + (at - deep) * plane, at) for at in [lax.rem(deep + step, planes) for step in range(1, planes)]]

    def remote(src, dst, send, recv, peer):
        return pltpu.make_async_remote_copy(
            src_ref=src, dst_ref=dst, send_sem=send, recv_sem=recv, device_id=(peer,), device_id_type=MESH
        )

    def coarse_cols(at):
        return pl.ds(pl.multiple_of(at * (plane * 16), plane * 16), plane * 16)

    load_coarse = pltpu.make_async_copy(coarse_hbm.at[:, coarse_cols(deep)], coarse_raw.at[deep], load_sem.at[2])
    load_neum = pltpu.make_async_copy(neum_hbm.at[0], raw.at[0], load_sem.at[0])
    load_stiff = pltpu.make_async_copy(stiff_hbm.at[0], raw.at[1], load_sem.at[1])
    load_neum.start()
    load_coarse.start()
    load_stiff.start()

    barrier = pltpu.get_barrier_semaphore()
    everyone = [peer for peer, _ in flat_others + deep_others] + list(sides)
    for peer in everyone:
        pl.semaphore_signal(barrier, inc=1, device_id=(peer,), device_id_type=MESH)
    live = jnp.concatenate([iota((1, width), 1) < len_ref[0, block] for block in range(faces)], axis=1)
    weight = jnp.concatenate([jnp.where(live, 0.5, 1.0), jnp.ones((1, ndof - shared), F32)], axis=1)

    columns = jnp.concatenate([index_ref[0].astype(F32), jnp.zeros((8 - faces, width), F32)], axis=0).T
    for block in range(faces):
        hit = columns[:, block:block + 1].astype(jnp.int32) == iota((width, ndof), 1)
        perm[block * width:(block + 1) * width, :] = jnp.where(hit, 1.0, 0.0).astype(BF16)
    loads_cat = jnp.concatenate(thirds(loads_ref[0]), axis=0)
    first = three(dot_nt(loads_cat, perm[:shared, :]), cases)
    pl.semaphore_wait(barrier, len(everyone))

    def face_copy(kind, block):
        pair = block ^ 1
        return remote(
            face_out.at[kind, block], face_in.at[kind, pair], face_send.at[kind, block], face_recv.at[kind, pair],
            sides[block],
        )

    def start_faces(kind, value):
        for block in range(faces):
            face_out[kind, block] = value[:, block * width:(block + 1) * width]
        for block in range(faces):
            face_copy(kind, block).start()

    def wait_faces(kind):
        for block in range(faces):
            face_copy(kind, block).wait_send()
        for block in range(faces):
            face_copy(kind, block).wait_recv()
        got = jnp.concatenate([face_in[kind, block] for block in range(faces)], axis=1)
        return jnp.where(live, got, 0.0)

    def add_faces(value, incoming):
        return jnp.concatenate([value[:, :shared] + incoming, value[:, shared:]], axis=1)

    def product(value, mat_hi, mat_lo, start, stop):
        high, low = halves(value)
        first_part = dot(jnp.concatenate([high, low], axis=0), mat_hi[:, start:stop])
        return first_part[:cases] + first_part[cases:] + dot(high, mat_lo[:, start:stop])

    def push(kind, turn, others, src_of, dst, here, send, recv):
        return [
            remote(src_of(at), dst.at[turn, here], send.at[kind, turn, step], recv.at[kind, turn, here], peer)
            for step, (peer, at) in enumerate(others)
        ]

    def pull(kind, turn, others, src_of, dst, send, recv):
        return [
            remote(src_of(at), dst.at[turn, at], send.at[kind, turn, step], recv.at[kind, turn, at], peer)
            for step, (peer, at) in enumerate(others)
        ]

    def start_all(*args):
        for copy in push(*args):
            copy.start()

    def wait_all(kind, turn, others, src_of, dst, send, recv):
        for copy in pull(kind, turn, others, src_of, dst, send, recv):
            copy.wait_send()
        for copy in pull(kind, turn, others, src_of, dst, send, recv):
            copy.wait_recv()

    def coarse_of(scaled):
        high, low = halves(scaled)
        return dot_nt(basis[:32, :scaled.shape[1]], jnp.concatenate([high, low], axis=0))

    def start_gather(turn, out):
        value = out[:16] + flip(out[:16]) + out[16:]
        own = jnp.where(left_half, value[:8], flip(value[8:]))
        gather_own[...] = own
        gather[turn, col] = own
        start_all(0, turn, flat_others, lambda at: gather_own, gather, col, flat_send, flat_recv)

    def start_spread(turn):
        wait_all(0, turn, flat_others, lambda at: gather_own, gather, flat_send, flat_recv)
        packed = gather[turn]
        turned = flip(packed)
        both = jnp.concatenate(
            [jnp.where(left_half, packed, turned), jnp.where(left_half, turned, packed)], axis=1
        ).reshape(plane * 16, wide)
        high = both.astype(BF16).astype(F32)
        right = jnp.where(left_half, high, both - high).astype(BF16)
        out = dot(coarse_cat[...], right)
        lines = planes * 16
        value = out[:lines] + flip(out[:lines]) + out[lines:]
        value = value.reshape(planes, 2, 8, wide)
        spread_out[...] = jnp.where(left_half, value[:, 0], flip(value[:, 1]))
        spread[turn, deep] = spread_out[deep]
        start_all(0, turn, deep_others, lambda at: spread_out.at[at], spread, deep, deep_send, deep_recv)

    def wait_spread(turn):
        wait_all(0, turn, deep_others, lambda at: spread_out.at[at], spread, deep_send, deep_recv)
        return jnp.sum(spread[turn], axis=0)

    def coarse_rows(packed):
        both = jnp.concatenate([packed, flip(packed)], axis=0)
        high = both.astype(BF16).astype(F32)
        stacked = jnp.concatenate([high, high, both - high, jnp.zeros_like(high)], axis=0)
        return stacked.T[:cases].astype(BF16)

    def row_sum(value):
        part = value[:, :128]
        for block in range(128, ndof, 128):
            part = part + value[:, block:block + 128]
        part = jnp.sum(part.T, axis=0, keepdims=True)
        return jnp.concatenate([part, part], axis=1)

    def as_column(scalar_row):
        return jnp.broadcast_to(scalar_row, (8, wide)).T[:cases, :1]

    def start_sums(turn, parts):
        own = jnp.concatenate(parts, axis=1)
        sums_own[...] = own
        sums[turn, col] = own
        start_all(1, turn, flat_others, lambda at: sums_own, sums, col, flat_send, flat_recv)

    def lift_sums(turn):
        wait_all(1, turn, flat_others, lambda at: sums_own, sums, flat_send, flat_recv)
        own = jnp.sum(sums[turn], axis=0)
        tops_own[...] = own
        tops[turn, deep] = own
        start_all(1, turn, deep_others, lambda at: tops_own, tops, deep, deep_send, deep_recv)

    def wait_sums(turn):
        wait_all(1, turn, deep_others, lambda at: tops_own, tops, deep_send, deep_recv)
        total = jnp.sum(tops[turn], axis=0)
        return total[:, :wide], total[:, wide:2 * wide], total[:, 2 * wide:]

    tall = 256

    def turn(which, start, stop):
        def block(step, carry):
            here = pl.ds(pl.multiple_of(step * tall, tall), tall)
            high, low = halves(raw[which, here, :])
            both = dot_nt(jnp.concatenate([high, low], axis=0), perm[start:stop, :]).astype(BF16)
            turned_hi[here, start:stop] = both[:tall]
            turned_lo[here, start:stop] = both[tall:]
            return carry

        lax.fori_loop(0, ndof // tall, block, 0)

    def settle(out_hi, out_lo, start, stop, begin, end):
        def block(step, carry):
            here = pl.ds(pl.multiple_of(step * tall, tall), tall)
            pick = perm[here, :]
            out_hi[here, start:stop] = dot(pick, turned_hi[:, start:stop]).astype(BF16)
            out_lo[here, start:stop] = dot(pick, turned_lo[:, start:stop]).astype(BF16)
            return carry

        lax.fori_loop(begin, end, block, 0)

    start_faces(1, first)
    for step, (peer, at) in enumerate(deep_others):
        remote(
            coarse_hbm.at[:, coarse_cols(at)], coarse_raw.at[deep], deep_send.at[2, 0, step], deep_recv.at[2, 0, deep], peer
        ).start()
    sol_ref[...] = jnp.zeros_like(sol_ref)
    direction_ref[...] = jnp.zeros_like(direction_ref)
    image_ref[...] = jnp.zeros_like(image_ref)
    scalars[...] = jnp.ones_like(scalars)

    taken = dot(jnp.ones((16, shared), BF16), perm[:shared, :])[:8]
    free = (1.0 - taken).astype(BF16)
    rank = jnp.zeros((8, ndof), F32)
    for block in range(0, ndof, 128):
        before = jnp.where(iota((128, ndof), 0) + block < iota((128, ndof), 1), 1.0, 0.0).astype(BF16)
        rank = rank + dot(free[:, block:block + 128], before)
    place = jnp.where(taken[:1] > 0.5, -1.0, rank[:1]).astype(jnp.int32)
    for block in range(0, ndof - shared, 128):
        hit = place == iota((128, ndof), 0) + block
        perm[shared + block:shared + block + 128, :] = jnp.where(hit, 1.0, 0.0).astype(BF16)
    rest = three(dot_nt(loads_cat, perm[shared:, :]), cases)
    basis_hi, basis_lo = halves(three(dot_nt(jnp.concatenate(thirds(basis_ref[0]), axis=0), perm[...]), 16))
    basis[...] = jnp.concatenate(
        [basis_hi, basis_lo, basis_hi, basis_lo, basis_hi, jnp.zeros_like(basis_hi)], axis=0
    )
    load_neum.wait()
    turn(0, 0, shared)
    resid = jnp.concatenate([first + wait_faces(1), rest], axis=1)
    start_gather(0, coarse_of(weight * resid))
    res_ref[...] = resid
    load_coarse.wait()
    for receive in (False, True):
        for step, (peer, at) in enumerate(deep_others):
            copy = remote(
                coarse_hbm.at[:, coarse_cols(at)], coarse_raw.at[at], deep_send.at[2, 0, step], deep_recv.at[2, 0, at], peer
            )
            if receive:
                copy.wait_recv()
            else:
                copy.wait_send()
    coarse_hi, coarse_lo = halves(coarse_raw[...].reshape(planes * 16, plane * 16))
    coarse_cat[...] = jnp.concatenate([coarse_hi, coarse_lo], axis=0)
    turn(0, shared, ndof)
    settle(neum_hi, neum_lo, 0, shared, 0, ndof // tall)
    start_spread(0)
    settle(neum_hi, neum_lo, shared, ndof, 0, ndof // tall)
    local_ref[...] = product(weight * res_ref[...], neum_hi, neum_lo, 0, ndof)
    load_stiff.wait()
    coarse_state[0] = wait_spread(0)
    coarse_state[1] = jnp.zeros_like(coarse_state[1])

    def unturn(one, two):
        both = three(dot(jnp.concatenate(thirds(jnp.concatenate([one, two], axis=0)), axis=0), perm[...]), 2 * cases)
        return [both[:cases], both[cases:]]

    def iterate(step, last):
        now, later = (step % 2, (step + 1) % 2) if last else (lax.rem(step, 2), lax.rem(step + 1, 2))
        coarse_part = coarse_rows(coarse_state[0])
        near_sol = weight[:, :shared] * (local_ref[:, :shared] + dot(coarse_part, basis[32:, :shared]))
        start_faces(0, near_sol)
        half_sol = jnp.concatenate([near_sol, local_ref[:, shared:] + dot(coarse_part, basis[32:, shared:])], axis=1)
        rz_part = row_sum(half_sol * res_ref[...])

        if not last:
            @pl.when(step == 0)
            def _():
                turn(1, 0, shared)
                settle(stiff_hi, stiff_lo, 0, shared, 0, ndof // tall)

        precond = add_faces(half_sol, wait_faces(0))
        near = product(precond, stiff_hi, stiff_lo, 0, shared)
        start_faces(1, near)

        if not last:
            @pl.when(step == 0)
            def _():
                turn(1, shared, ndof)
                settle(stiff_hi, stiff_lo, shared, ndof, 0, ndof // tall)

        image = jnp.concatenate([near, product(precond, stiff_hi, stiff_lo, shared, ndof)], axis=1)
        zz_part = row_sum(precond * image)
        zq_part = row_sum(weight * precond * image_ref[...])
        start_sums(now, [rz_part, zz_part, zq_part])
        if last:
            kept = unturn(sol_ref[...], precond) + unturn(direction_ref[...], res_ref[...])
            image = add_faces(image, wait_faces(1))
        else:
            coarse_own = coarse_of(weight * image)
            incoming = wait_faces(1)
            coarse_near = coarse_of(0.5 * incoming)
            start_gather(later, coarse_own + coarse_near)
            image = add_faces(image, incoming)
        lift_sums(now)
        if last:
            kept = kept + unturn(image, image_ref[...])
        else:
            start_spread(later)
        rz, zz, zq = wait_sums(now)
        beta = jnp.where(step > 0, rz / scalars[0:1], 0.0)
        denom = zz + beta * (2.0 * zq) + beta * (beta * jnp.where(step > 0, scalars[1:2], 0.0))
        alpha = rz / denom
        slope, length = as_column(beta), as_column(alpha)
        if last:
            sol_out[...] = kept[0] + length * (kept[1] + slope * kept[2])
            res_out[...] = kept[3] - length * (kept[4] + slope * kept[5])
            return
        direction = precond + slope * direction_ref[...]
        image = image + slope * image_ref[...]
        resid = res_ref[...] - length * image
        sol_ref[...] = sol_ref[...] + length * direction
        res_ref[...] = resid
        direction_ref[...] = direction
        image_ref[...] = image
        scalars[0:1] = rz
        scalars[1:2] = denom
        local_ref[...] = product(weight * resid, neum_hi, neum_lo, 0, ndof)
        coarse_image = wait_spread(later) + beta * coarse_state[1]
        coarse_state[1] = coarse_image
        coarse_state[0] = coarse_state[0] - alpha * coarse_image

    def body(step, carry):
        iterate(step, False)
        return carry

    lax.fori_loop(0, ITERS - 1, body, 0)
    iterate(ITERS - 1, True)


def hand_over(sol_ref, res_ref, sol_out, res_out):
    sol_out[0] = sol_ref[...]
    res_out[0] = res_ref[...]


def local(sizes, cycle, stiffness, neumann_inv, coarse_basis, coarse_inv, loads, face_index, face_len):
    cases, ndof = loads.shape[1:]
    faces, width = face_index.shape[1:]
    planes, plane = sizes
    wide = 2 * cases
    anywhere = pl.BlockSpec(memory_space=pl.ANY)
    inside = pl.BlockSpec(memory_space=pltpu.VMEM)
    square = pltpu.VMEM((ndof, ndof), BF16)
    plain = pltpu.VMEM((cases, ndof), F32)
    whole = jax.ShapeDtypeStruct((1, cases, ndof), F32)
    flat = jax.ShapeDtypeStruct((cases, ndof), F32)
    results = pl.pallas_call(
        functools.partial(kernel, sizes, cycle),
        out_shape=(flat, flat),
        in_specs=[anywhere, anywhere, inside, anywhere, inside, inside, pl.BlockSpec(memory_space=pltpu.SMEM)],
        out_specs=(inside, inside),
        scratch_shapes=[
            pltpu.VMEM((2, ndof, ndof), F32),
            square, square, square, square, square, square, square,
            pltpu.VMEM((96, ndof), BF16),
            plain, plain,
            pltpu.VMEM((planes, 16, plane * 16), F32),
            pltpu.VMEM((2 * planes * 16, plane * 16), BF16),
            pltpu.VMEM((cases, ndof), F32),
            pltpu.VMEM((cases, ndof), F32),
            pltpu.VMEM((cases, ndof), F32),
            pltpu.VMEM((8, wide), F32),
            pltpu.VMEM((2, 8, wide), F32),
            pltpu.VMEM((2, faces, cases, width), F32),
            pltpu.VMEM((2, faces, cases, width), F32),
            pltpu.VMEM((2, plane, 8, wide), F32),
            pltpu.VMEM((8, wide), F32),
            pltpu.VMEM((2, planes, 8, wide), F32),
            pltpu.VMEM((planes, 8, wide), F32),
            pltpu.VMEM((2, plane, 1, 3 * wide), F32),
            pltpu.VMEM((1, 3 * wide), F32),
            pltpu.VMEM((2, planes, 1, 3 * wide), F32),
            pltpu.VMEM((1, 3 * wide), F32),
            pltpu.SemaphoreType.DMA((3,)),
            pltpu.SemaphoreType.DMA((2, faces)),
            pltpu.SemaphoreType.DMA((2, faces)),
            pltpu.SemaphoreType.DMA((2, 2, plane)),
            pltpu.SemaphoreType.DMA((2, 2, plane)),
            pltpu.SemaphoreType.DMA((3, 2, planes)),
            pltpu.SemaphoreType.DMA((3, 2, planes)),
        ],
        compiler_params=pltpu.CompilerParams(
            collective_id=0, has_side_effects=True, vmem_limit_bytes=56 * 1024 * 1024
        ),
        name="solve",
    )(stiffness, neumann_inv, coarse_basis, coarse_inv, loads, face_index, face_len)
    return pl.pallas_call(
        hand_over, out_shape=(whole, whole), in_specs=[inside] * 2, out_specs=(inside, inside), name="hand_over"
    )(*results)


def solution(mesh, plane=PLANE, cycle=CYCLE):
    subs = mesh.shape["sub"]
    placed = (
        P("sub", None, None),
        P("sub", None, None),
        P("sub", None, None),
        P("sub", None),
        P("sub", None, None),
        P("sub", None, None),
        P("sub", None),
    )
    return jax.shard_map(
        functools.partial(local, (subs // plane, plane), cycle),
        mesh=mesh,
        in_specs=placed,
        out_specs=(P("sub", None, None), P("sub", None, None)),
        check_vma=False,
    )
```

```python
import functools

import jax
import jax.numpy as jnp
from jax import lax
from jax.experimental import pallas as pl
from jax.experimental.pallas import tpu as pltpu
from jax.sharding import PartitionSpec as P

CYCLE = 16
ITERS = 4
PLANE = 32
MESH = pl.DeviceIdType.MESH
F32 = jnp.float32
BF16 = jnp.bfloat16


def halves(value):
    high = value.astype(BF16)
    return high, (value - high.astype(F32)).astype(BF16)


def thirds(value):
    high = value.astype(BF16)
    rest = value - high.astype(F32)
    mid = rest.astype(BF16)
    return high, mid, (rest - mid.astype(F32)).astype(BF16)


def dot(left, right):
    return jnp.dot(left, right, preferred_element_type=F32)


def dot_nt(left, right):
    return lax.dot_general(left, right, (((1,), (1,)), ((), ())), preferred_element_type=F32)


def iota(shape, dim):
    return lax.broadcasted_iota(jnp.int32, shape, dim)


def three(parts, cases):
    return parts[:cases] + parts[cases:2 * cases] + parts[2 * cases:]


def kernel(
    sizes, cycle, stiff_hbm, neum_hbm, basis_ref, coarse_hbm, loads_ref, index_ref, len_ref, sol_out, res_out,
    raw, perm, turned_hi, turned_lo, neum_hi, neum_lo, stiff_hi, stiff_lo, basis, sol_ref, res_ref,
    coarse_raw, coarse_cat, image_ref, direction_ref, local_ref, scalars, coarse_state, face_out, face_in,
    gather, gather_own, spread, spread_out, sums, sums_own, tops, tops_own,
    side_basis, side_mix, side_wide, side_out, side_in,
    load_sem, face_send, face_recv, side_send, side_recv, flat_send, flat_recv, deep_send, deep_recv,
):
    planes, plane = sizes
    subs = planes * plane
    cases, ndof = loads_ref.shape[1:]
    faces, width = face_in.shape[1], face_in.shape[3]
    shared = faces * width
    wide = 2 * cases
    me = lax.axis_index("sub")
    deep, col = me // plane, lax.rem(me, plane)
    left_half = iota((1, wide), 1) < cases

    def flip(value):
        return pltpu.roll(value, cases, axis=value.ndim - 1)

    sides = (
        lax.rem(me + subs - 1, subs), lax.rem(me + 1, subs),
        lax.rem(me + subs - cycle, subs), lax.rem(me + cycle, subs),
    )
    span = min(4, plane // 2)
    tall_y = plane // (2 * span)
    at_y, at_x, at_core = col // (2 * span), lax.rem(col // 2, span), lax.rem(col, 2)

    def hops(step, length):
        return min(step, length - step)

    offsets = [(y, x, c) for y in range(tall_y) for x in range(span) for c in range(2)][1:]
    offsets.sort(key=lambda d: -hops(d[0], tall_y) - hops(d[1], span))
    flat_places = [
        lax.rem(at_y + y, tall_y) * (2 * span) + lax.rem(at_x + x, span) * 2 + lax.rem(at_core + c, 2)
        for y, x, c in offsets
    ]
    deep_steps = sorted(range(1, planes), key=lambda step: -hops(step, planes))
    flat_others = [(me - col + at, at) for at in flat_places]
    deep_others = [(me + (at - deep) * plane, at) for at in [lax.rem(deep + step, planes) for step in deep_steps]]

    def remote(src, dst, send, recv, peer):
        return pltpu.make_async_remote_copy(
            src_ref=src, dst_ref=dst, send_sem=send, recv_sem=recv, device_id=(peer,), device_id_type=MESH
        )

    def coarse_cols(at):
        return pl.ds(pl.multiple_of(at * (plane * 16), plane * 16), plane * 16)

    load_coarse = pltpu.make_async_copy(coarse_hbm.at[:, coarse_cols(deep)], coarse_raw.at[deep], load_sem.at[2])
    load_neum = pltpu.make_async_copy(neum_hbm.at[0], raw.at[0], load_sem.at[0])
    load_stiff = pltpu.make_async_copy(stiff_hbm.at[0], raw.at[1], load_sem.at[1])
    load_neum.start()
    load_coarse.start()
    load_stiff.start()

    barrier = pltpu.get_barrier_semaphore()
    everyone = [peer for peer, _ in flat_others + deep_others] + list(sides)
    for peer in everyone:
        pl.semaphore_signal(barrier, inc=1, device_id=(peer,), device_id_type=MESH)
    live = jnp.concatenate([iota((1, width), 1) < len_ref[0, block] for block in range(faces)], axis=1)
    weight = jnp.concatenate([jnp.where(live, 0.5, 1.0), jnp.ones((1, ndof - shared), F32)], axis=1)

    columns = jnp.concatenate([index_ref[0].astype(F32), jnp.zeros((8 - faces, width), F32)], axis=0).T
    for block in range(faces):
        hit = columns[:, block:block + 1].astype(jnp.int32) == iota((width, ndof), 1)
        perm[block * width:(block + 1) * width, :] = jnp.where(hit, 1.0, 0.0).astype(BF16)
    loads_cat = jnp.concatenate(thirds(loads_ref[0]), axis=0)
    first = three(dot_nt(loads_cat, perm[:shared, :]), cases)
    pl.semaphore_wait(barrier, len(everyone))

    def face_copy(kind, block):
        pair = block ^ 1
        return remote(
            face_out.at[kind, block], face_in.at[kind, pair], face_send.at[kind, block], face_recv.at[kind, pair],
            sides[block],
        )

    def start_faces(kind, value):
        for block in range(faces):
            face_out[kind, block] = value[:, block * width:(block + 1) * width]
        for block in range(faces):
            face_copy(kind, block).start()

    def wait_faces(kind):
        for block in range(faces):
            face_copy(kind, block).wait_send()
        for block in range(faces):
            face_copy(kind, block).wait_recv()
        got = jnp.concatenate([face_in[kind, block] for block in range(faces)], axis=1)
        return jnp.where(live, got, 0.0)

    def side_copy(kind, block):
        pair = block ^ 1
        source, target = (
            (side_basis.at[0, block], side_basis.at[1, pair]) if kind == 2
            else (side_out.at[kind, block], side_in.at[kind, pair])
        )
        return remote(source, target, side_send.at[kind, block], side_recv.at[kind, pair], sides[block])

    def start_sides(kind):
        for block in range(faces):
            side_copy(kind, block).start()

    def wait_sides(kind):
        for block in range(faces):
            side_copy(kind, block).wait_send()
        for block in range(faces):
            side_copy(kind, block).wait_recv()

    def add_faces(value, incoming):
        return jnp.concatenate([value[:, :shared] + incoming, value[:, shared:]], axis=1)

    def product(value, mat_hi, mat_lo, start, stop):
        high, low = halves(value)
        first_part = dot(jnp.concatenate([high, low], axis=0), mat_hi[:, start:stop])
        return first_part[:cases] + first_part[cases:] + dot(high, mat_lo[:, start:stop])

    def push(kind, turn, others, src_of, dst, here, send, recv):
        return [
            remote(src_of(at), dst.at[turn, here], send.at[kind, turn, step], recv.at[kind, turn, here], peer)
            for step, (peer, at) in enumerate(others)
        ]

    def pull(kind, turn, others, src_of, dst, send, recv):
        return [
            remote(src_of(at), dst.at[turn, at], send.at[kind, turn, step], recv.at[kind, turn, at], peer)
            for step, (peer, at) in enumerate(others)
        ]

    def start_all(*args):
        for copy in push(*args):
            copy.start()

    def wait_received(*args):
        for copy in pull(*args):
            copy.wait_recv()

    def wait_sent(*args):
        for copy in pull(*args):
            copy.wait_send()

    def coarse_of(scaled):
        high, low = halves(scaled)
        return dot_nt(basis[:32, :scaled.shape[1]], jnp.concatenate([high, low], axis=0))

    def pack(out):
        value = out[:16] + flip(out[:16]) + out[16:]
        return jnp.where(left_half, value[:8], flip(value[8:]))

    def start_gather(turn, own):
        gather_own[...] = own
        gather[turn, col] = own
        start_all(0, turn, flat_others, lambda at: gather_own, gather, col, flat_send, flat_recv)

    def start_spread(turn):
        wait_received(0, turn, flat_others, lambda at: gather_own, gather, flat_send, flat_recv)
        packed = gather[turn]
        turned = flip(packed)
        both = jnp.concatenate(
            [jnp.where(left_half, packed, turned), jnp.where(left_half, turned, packed)], axis=1
        ).reshape(plane * 16, wide)
        high = both.astype(BF16).astype(F32)
        right = jnp.where(left_half, high, both - high).astype(BF16)
        out = dot(coarse_cat[...], right)
        lines = planes * 16
        value = out[:lines] + flip(out[:lines]) + out[lines:]
        value = value.reshape(planes, 2, 8, wide)
        spread_out[...] = jnp.where(left_half, value[:, 0], flip(value[:, 1]))
        spread[turn, deep] = spread_out[deep]
        start_all(0, turn, deep_others, lambda at: spread_out.at[at], spread, deep, deep_send, deep_recv)
        wait_sent(0, turn, flat_others, lambda at: gather_own, gather, flat_send, flat_recv)

    def wait_spread(turn):
        wait_sent(0, turn, deep_others, lambda at: spread_out.at[at], spread, deep_send, deep_recv)
        wait_received(0, turn, deep_others, lambda at: spread_out.at[at], spread, deep_send, deep_recv)
        return jnp.sum(spread[turn], axis=0)

    def coarse_stack(packed):
        both = jnp.concatenate([packed, flip(packed)], axis=0)
        high = both.astype(BF16).astype(F32)
        return jnp.concatenate([high, high, both - high, jnp.zeros_like(high)], axis=0)

    def coarse_rows(*packed):
        return jnp.concatenate([coarse_stack(one) for one in packed], axis=0).T[:cases].astype(BF16)

    def row_sum(value):
        part = value[:, :128]
        for block in range(128, ndof, 128):
            part = part + value[:, block:block + 128]
        part = jnp.sum(part.T, axis=0, keepdims=True)
        return jnp.concatenate([part, part], axis=1)

    def as_column(scalar_row):
        return jnp.broadcast_to(scalar_row, (8, wide)).T[:cases, :1]

    def start_sums(turn, parts):
        own = jnp.concatenate(parts, axis=1)
        sums_own[...] = own
        sums[turn, col] = own
        start_all(1, turn, flat_others, lambda at: sums_own, sums, col, flat_send, flat_recv)

    def lift_sums(turn):
        wait_received(1, turn, flat_others, lambda at: sums_own, sums, flat_send, flat_recv)
        own = jnp.sum(sums[turn], axis=0)
        tops_own[...] = own
        tops[turn, deep] = own
        start_all(1, turn, deep_others, lambda at: tops_own, tops, deep, deep_send, deep_recv)
        wait_sent(1, turn, flat_others, lambda at: sums_own, sums, flat_send, flat_recv)

    def wait_sums(turn):
        wait_sent(1, turn, deep_others, lambda at: tops_own, tops, deep_send, deep_recv)
        wait_received(1, turn, deep_others, lambda at: tops_own, tops, deep_send, deep_recv)
        total = jnp.sum(tops[turn], axis=0)
        return total[:, :wide], total[:, wide:2 * wide], total[:, 2 * wide:]

    tall = 256

    def turn(which, start, stop):
        def block(step, carry):
            here = pl.ds(pl.multiple_of(step * tall, tall), tall)
            high, low = halves(raw[which, here, :])
            both = dot_nt(jnp.concatenate([high, low], axis=0), perm[start:stop, :]).astype(BF16)
            turned_hi[here, start:stop] = both[:tall]
            turned_lo[here, start:stop] = both[tall:]
            return carry

        lax.fori_loop(0, ndof // tall, block, 0)

    def settle(out_hi, out_lo, start, stop, begin, end):
        def block(step, carry):
            here = pl.ds(pl.multiple_of(step * tall, tall), tall)
            pick = perm[here, :]
            out_hi[here, start:stop] = dot(pick, turned_hi[:, start:stop]).astype(BF16)
            out_lo[here, start:stop] = dot(pick, turned_lo[:, start:stop]).astype(BF16)
            return carry

        lax.fori_loop(begin, end, block, 0)

    start_faces(1, first)
    for step, (peer, at) in enumerate(deep_others):
        remote(
            coarse_hbm.at[:, coarse_cols(at)], coarse_raw.at[deep], deep_send.at[2, 0, step], deep_recv.at[2, 0, deep], peer
        ).start()
    sol_ref[...] = jnp.zeros_like(sol_ref)
    direction_ref[...] = jnp.zeros_like(direction_ref)
    image_ref[...] = jnp.zeros_like(image_ref)
    scalars[...] = jnp.ones_like(scalars)

    taken = dot(jnp.ones((16, shared), BF16), perm[:shared, :])[:8]
    free = (1.0 - taken).astype(BF16)
    rank = jnp.zeros((8, ndof), F32)
    for block in range(0, ndof, 128):
        before = jnp.where(iota((128, ndof), 0) + block < iota((128, ndof), 1), 1.0, 0.0).astype(BF16)
        rank = rank + dot(free[:, block:block + 128], before)
    place = jnp.where(taken[:1] > 0.5, -1.0, rank[:1]).astype(jnp.int32)
    for block in range(0, ndof - shared, 128):
        hit = place == iota((128, ndof), 0) + block
        perm[shared + block:shared + block + 128, :] = jnp.where(hit, 1.0, 0.0).astype(BF16)
    rest = three(dot_nt(loads_cat, perm[shared:, :]), cases)
    basis_own = three(dot_nt(jnp.concatenate(thirds(basis_ref[0]), axis=0), perm[...]), 16)
    for block in range(faces):
        side_basis[0, block] = basis_own[:, block * width:(block + 1) * width]
    start_sides(2)
    side_mix[...] = jnp.zeros_like(side_mix)
    side_wide[...] = jnp.zeros_like(side_wide)
    basis_hi, basis_lo = halves(basis_own)
    basis[...] = jnp.concatenate(
        [basis_hi, basis_lo, basis_hi, basis_lo, basis_hi, jnp.zeros_like(basis_hi)], axis=0
    )
    load_neum.wait()
    turn(0, 0, ndof)
    resid = jnp.concatenate([first + wait_faces(1), rest], axis=1)
    start_gather(0, pack(coarse_of(weight * resid)))
    res_ref[...] = resid
    load_coarse.wait()
    for receive in (False, True):
        for step, (peer, at) in enumerate(deep_others):
            copy = remote(
                coarse_hbm.at[:, coarse_cols(at)], coarse_raw.at[at], deep_send.at[2, 0, step], deep_recv.at[2, 0, at], peer
            )
            if receive:
                copy.wait_recv()
            else:
                copy.wait_send()
    coarse_hi, coarse_lo = halves(coarse_raw[...].reshape(planes * 16, plane * 16))
    coarse_cat[...] = jnp.concatenate([coarse_hi, coarse_lo], axis=0)
    settle(neum_hi, neum_lo, 0, ndof, 0, ndof // tall)
    start_spread(0)
    local_ref[...] = product(weight * res_ref[...], neum_hi, neum_lo, 0, ndof)
    start_faces(0, weight[:, :shared] * local_ref[:, :shared])
    wait_sides(2)
    for block in range(faces):
        near_basis = side_basis[1, block] * jnp.where(live[:, block * width:(block + 1) * width], 0.5, 0.0)
        high, low = halves(near_basis)
        at = slice(block * width, (block + 1) * width)
        side_mix[32 * block:32 * (block + 1), at] = jnp.concatenate([high, low], axis=0)
        side_wide[64 * block:64 * (block + 1), at] = jnp.concatenate([high, low, high, jnp.zeros_like(high)], axis=0)
    load_stiff.wait()
    turn(1, 0, shared)
    coarse_first = wait_spread(0)
    coarse_state[0] = coarse_first
    for block in range(faces):
        side_out[0, block] = coarse_first
    start_sides(0)
    coarse_state[1] = jnp.zeros_like(coarse_state[1])

    def unturn(one, two):
        both = three(dot(jnp.concatenate(thirds(jnp.concatenate([one, two], axis=0)), axis=0), perm[...]), 2 * cases)
        return [both[:cases], both[cases:]]

    def iterate(step, last):
        now, later = (step % 2, (step + 1) % 2) if last else (lax.rem(step, 2), lax.rem(step + 1, 2))
        coarse_part = coarse_rows(coarse_state[0])
        half_sol = weight * (local_ref[...] + dot(coarse_part, basis[32:, :]))
        rz_part = row_sum(half_sol * res_ref[...])

        if not last:
            @pl.when(step == 0)
            def _():
                settle(stiff_hi, stiff_lo, 0, shared, 0, ndof // tall)

        incoming = wait_faces(0)
        wait_sides(0)
        incoming = incoming + dot(coarse_rows(*[side_in[0, block] for block in range(faces)]), side_wide[...])
        precond = add_faces(half_sol, incoming)
        near = product(precond, stiff_hi, stiff_lo, 0, shared)
        if not last:
            high, low = halves(near)
            mixed = dot_nt(side_mix[...], jnp.concatenate([high, low], axis=0))
            for block in range(faces):
                side_out[1, block] = pack(mixed[32 * block:32 * (block + 1)])
            start_sides(1)
        start_faces(1, near)

        if not last:
            @pl.when(step == 0)
            def _():
                turn(1, shared, ndof)
                settle(stiff_hi, stiff_lo, shared, ndof, 0, ndof // tall)

        image = jnp.concatenate([near, product(precond, stiff_hi, stiff_lo, shared, ndof)], axis=1)
        zz_part = row_sum(precond * image)
        zq_part = row_sum(weight * precond * image_ref[...])
        start_sums(now, [rz_part, zz_part, zq_part])
        if last:
            kept = unturn(sol_ref[...], precond) + unturn(direction_ref[...], res_ref[...])
            image = add_faces(image, wait_faces(1))
        else:
            coarse_own = pack(coarse_of(weight * image))
            wait_sides(1)
            start_gather(later, coarse_own + jnp.sum(side_in[1], axis=0))
            image = add_faces(image, wait_faces(1))
        lift_sums(now)
        if last:
            kept = kept + unturn(image, image_ref[...])
        else:
            start_spread(later)
        rz, zz, zq = wait_sums(now)
        beta = jnp.where(step > 0, rz / scalars[0:1], 0.0)
        denom = zz + beta * (2.0 * zq) + beta * (beta * jnp.where(step > 0, scalars[1:2], 0.0))
        alpha = rz / denom
        slope, length = as_column(beta), as_column(alpha)
        if last:
            sol_out[...] = kept[0] + length * (kept[1] + slope * kept[2])
            res_out[...] = kept[3] - length * (kept[4] + slope * kept[5])
            return
        direction = precond + slope * direction_ref[...]
        image = image + slope * image_ref[...]
        resid = res_ref[...] - length * image
        sol_ref[...] = sol_ref[...] + length * direction
        res_ref[...] = resid
        direction_ref[...] = direction
        image_ref[...] = image
        scalars[0:1] = rz
        scalars[1:2] = denom
        local_next = product(weight * resid, neum_hi, neum_lo, 0, ndof)
        start_faces(0, weight[:, :shared] * local_next[:, :shared])
        local_ref[...] = local_next
        coarse_image = wait_spread(later) + beta * coarse_state[1]
        coarse_next = coarse_state[0] - alpha * coarse_image
        for block in range(faces):
            side_out[0, block] = coarse_next
        start_sides(0)
        coarse_state[1] = coarse_image
        coarse_state[0] = coarse_next

    def body(step, carry):
        iterate(step, False)
        return carry

    lax.fori_loop(0, ITERS - 1, body, 0)
    iterate(ITERS - 1, True)


def hand_over(sol_ref, res_ref, sol_out, res_out):
    sol_out[0] = sol_ref[...]
    res_out[0] = res_ref[...]


def local(sizes, cycle, stiffness, neumann_inv, coarse_basis, coarse_inv, loads, face_index, face_len):
    cases, ndof = loads.shape[1:]
    faces, width = face_index.shape[1:]
    planes, plane = sizes
    wide = 2 * cases
    anywhere = pl.BlockSpec(memory_space=pl.ANY)
    inside = pl.BlockSpec(memory_space=pltpu.VMEM)
    square = pltpu.VMEM((ndof, ndof), BF16)
    plain = pltpu.VMEM((cases, ndof), F32)
    whole = jax.ShapeDtypeStruct((1, cases, ndof), F32)
    flat = jax.ShapeDtypeStruct((cases, ndof), F32)
    results = pl.pallas_call(
        functools.partial(kernel, sizes, cycle),
        out_shape=(flat, flat),
        in_specs=[anywhere, anywhere, inside, anywhere, inside, inside, pl.BlockSpec(memory_space=pltpu.SMEM)],
        out_specs=(inside, inside),
        scratch_shapes=[
            pltpu.VMEM((2, ndof, ndof), F32),
            square, square, square, square, square, square, square,
            pltpu.VMEM((96, ndof), BF16),
            plain, plain,
            pltpu.VMEM((planes, 16, plane * 16), F32),
            pltpu.VMEM((2 * planes * 16, plane * 16), BF16),
            pltpu.VMEM((cases, ndof), F32),
            pltpu.VMEM((cases, ndof), F32),
            pltpu.VMEM((cases, ndof), F32),
            pltpu.VMEM((8, wide), F32),
            pltpu.VMEM((2, 8, wide), F32),
            pltpu.VMEM((2, faces, cases, width), F32),
            pltpu.VMEM((2, faces, cases, width), F32),
            pltpu.VMEM((2, plane, 8, wide), F32),
            pltpu.VMEM((8, wide), F32),
            pltpu.VMEM((2, planes, 8, wide), F32),
            pltpu.VMEM((planes, 8, wide), F32),
            pltpu.VMEM((2, plane, 1, 3 * wide), F32),
            pltpu.VMEM((1, 3 * wide), F32),
            pltpu.VMEM((2, planes, 1, 3 * wide), F32),
            pltpu.VMEM((1, 3 * wide), F32),
            pltpu.VMEM((2, faces, 16, width), F32),
            pltpu.VMEM((32 * faces, faces * width), BF16),
            pltpu.VMEM((64 * faces, faces * width), BF16),
            pltpu.VMEM((2, faces, 8, wide), F32),
            pltpu.VMEM((2, faces, 8, wide), F32),
            pltpu.SemaphoreType.DMA((3,)),
            pltpu.SemaphoreType.DMA((2, faces)),
            pltpu.SemaphoreType.DMA((2, faces)),
            pltpu.SemaphoreType.DMA((3, faces)),
            pltpu.SemaphoreType.DMA((3, faces)),
            pltpu.SemaphoreType.DMA((2, 2, plane)),
            pltpu.SemaphoreType.DMA((2, 2, plane)),
            pltpu.SemaphoreType.DMA((3, 2, planes)),
            pltpu.SemaphoreType.DMA((3, 2, planes)),
        ],
        compiler_params=pltpu.CompilerParams(
            collective_id=0, has_side_effects=True, vmem_limit_bytes=56 * 1024 * 1024
        ),
        name="solve",
    )(stiffness, neumann_inv, coarse_basis, coarse_inv, loads, face_index, face_len)
    return pl.pallas_call(
        hand_over, out_shape=(whole, whole), in_specs=[inside] * 2, out_specs=(inside, inside), name="hand_over"
    )(*results)


def solution(mesh, plane=PLANE, cycle=CYCLE):
    subs = mesh.shape["sub"]
    placed = (
        P("sub", None, None),
        P("sub", None, None),
        P("sub", None, None),
        P("sub", None),
        P("sub", None, None),
        P("sub", None, None),
        P("sub", None),
    )
    return jax.shard_map(
        functools.partial(local, (subs // plane, plane), cycle),
        mesh=mesh,
        in_specs=placed,
        out_specs=(P("sub", None, None), P("sub", None, None)),
        check_vma=False,
    )
```

```python
import functools

import jax
import jax.numpy as jnp
from jax import lax
from jax.experimental import pallas as pl
from jax.experimental.pallas import tpu as pltpu
from jax.sharding import PartitionSpec as P

CYCLE = 16
ITERS = 4
PLANE = 32
MESH = pl.DeviceIdType.MESH
F32 = jnp.float32
BF16 = jnp.bfloat16


def halves(value):
    high = value.astype(BF16)
    return high, (value - high.astype(F32)).astype(BF16)


def thirds(value):
    high = value.astype(BF16)
    rest = value - high.astype(F32)
    mid = rest.astype(BF16)
    return high, mid, (rest - mid.astype(F32)).astype(BF16)


def dot(left, right):
    return jnp.dot(left, right, preferred_element_type=F32)


def dot_nt(left, right):
    return lax.dot_general(left, right, (((1,), (1,)), ((), ())), preferred_element_type=F32)


def iota(shape, dim):
    return lax.broadcasted_iota(jnp.int32, shape, dim)


def three(parts, cases):
    return parts[:cases] + parts[cases:2 * cases] + parts[2 * cases:]


def kernel(
    sizes, cycle, stiff_hbm, neum_hbm, basis_ref, coarse_hbm, loads_ref, index_ref, len_ref, sol_out, res_out,
    raw, perm, turned_hi, turned_lo, neum_hi, neum_lo, stiff_hi, stiff_lo, basis, sol_ref, res_ref,
    coarse_raw, coarse_cat, image_ref, direction_ref, local_ref, slope_ref, edge_ref, scalars, coarse_state, face_out, face_in,
    gather, gather_own, spread, spread_out, sums, sums_own, tops, tops_own,
    side_basis, side_mix, side_wide, side_out, side_in,
    load_sem, face_send, face_recv, side_send, side_recv, flat_send, flat_recv, deep_send, deep_recv,
):
    planes, plane = sizes
    subs = planes * plane
    cases, ndof = loads_ref.shape[1:]
    faces, width = face_in.shape[1], face_in.shape[3]
    shared = faces * width
    wide = 2 * cases
    me = lax.axis_index("sub")
    deep, col = me // plane, lax.rem(me, plane)
    left_half = iota((1, wide), 1) < cases

    def flip(value):
        return pltpu.roll(value, cases, axis=value.ndim - 1)

    sides = (
        lax.rem(me + subs - 1, subs), lax.rem(me + 1, subs),
        lax.rem(me + subs - cycle, subs), lax.rem(me + cycle, subs),
    )
    span = min(4, plane // 2)
    tall_y = plane // (2 * span)
    at_y, at_x, at_core = col // (2 * span), lax.rem(col // 2, span), lax.rem(col, 2)

    def hops(step, length):
        return min(step, length - step)

    offsets = [(y, x, c) for y in range(tall_y) for x in range(span) for c in range(2)][1:]
    offsets.sort(key=lambda d: -hops(d[0], tall_y) - hops(d[1], span))
    flat_places = [
        lax.rem(at_y + y, tall_y) * (2 * span) + lax.rem(at_x + x, span) * 2 + lax.rem(at_core + c, 2)
        for y, x, c in offsets
    ]
    deep_steps = sorted(range(1, planes), key=lambda step: -hops(step, planes))
    flat_others = [(me - col + at, at) for at in flat_places]
    deep_others = [(me + (at - deep) * plane, at) for at in [lax.rem(deep + step, planes) for step in deep_steps]]

    def remote(src, dst, send, recv, peer):
        return pltpu.make_async_remote_copy(
            src_ref=src, dst_ref=dst, send_sem=send, recv_sem=recv, device_id=(peer,), device_id_type=MESH
        )

    def coarse_cols(at):
        return pl.ds(pl.multiple_of(at * (plane * 16), plane * 16), plane * 16)

    load_coarse = pltpu.make_async_copy(coarse_hbm.at[:, coarse_cols(deep)], coarse_raw.at[deep], load_sem.at[2])
    load_neum = pltpu.make_async_copy(neum_hbm.at[0], raw.at[0], load_sem.at[0])
    load_stiff = pltpu.make_async_copy(stiff_hbm.at[0], raw.at[1], load_sem.at[1])
    load_neum.start()
    load_coarse.start()
    load_stiff.start()

    barrier = pltpu.get_barrier_semaphore()
    everyone = [peer for peer, _ in flat_others + deep_others] + list(sides)
    for peer in everyone:
        pl.semaphore_signal(barrier, inc=1, device_id=(peer,), device_id_type=MESH)
    live = jnp.concatenate([iota((1, width), 1) < len_ref[0, block] for block in range(faces)], axis=1)
    weight = jnp.concatenate([jnp.where(live, 0.5, 1.0), jnp.ones((1, ndof - shared), F32)], axis=1)

    columns = jnp.concatenate([index_ref[0].astype(F32), jnp.zeros((8 - faces, width), F32)], axis=0).T
    for block in range(faces):
        hit = columns[:, block:block + 1].astype(jnp.int32) == iota((width, ndof), 1)
        perm[block * width:(block + 1) * width, :] = jnp.where(hit, 1.0, 0.0).astype(BF16)
    loads_cat = jnp.concatenate(thirds(loads_ref[0]), axis=0)
    first = three(dot_nt(loads_cat, perm[:shared, :]), cases)
    pl.semaphore_wait(barrier, len(everyone))

    def face_copy(kind, block):
        pair = block ^ 1
        return remote(
            face_out.at[kind, block], face_in.at[kind, pair], face_send.at[kind, block], face_recv.at[kind, pair],
            sides[block],
        )

    def start_faces(kind, value):
        for block in range(faces):
            face_out[kind, block] = value[:, block * width:(block + 1) * width]
        for block in range(faces):
            face_copy(kind, block).start()

    def wait_faces(kind):
        for block in range(faces):
            face_copy(kind, block).wait_send()
        for block in range(faces):
            face_copy(kind, block).wait_recv()
        got = jnp.concatenate([face_in[kind, block] for block in range(faces)], axis=1)
        return jnp.where(live, got, 0.0)

    def side_copy(kind, block):
        pair = block ^ 1
        source, target = (
            (side_basis.at[0, block], side_basis.at[1, pair]) if kind == 2
            else (side_out.at[kind, block], side_in.at[kind, pair])
        )
        return remote(source, target, side_send.at[kind, block], side_recv.at[kind, pair], sides[block])

    def start_sides(kind):
        for block in range(faces):
            side_copy(kind, block).start()

    def wait_sides(kind):
        for block in range(faces):
            side_copy(kind, block).wait_send()
        for block in range(faces):
            side_copy(kind, block).wait_recv()

    def add_faces(value, incoming):
        return jnp.concatenate([value[:, :shared] + incoming, value[:, shared:]], axis=1)

    def product(value, mat_hi, mat_lo, start, stop):
        high, low = halves(value)
        first_part = dot(jnp.concatenate([high, low], axis=0), mat_hi[:, start:stop])
        return first_part[:cases] + first_part[cases:] + dot(high, mat_lo[:, start:stop])

    def push(kind, turn, others, src_of, dst, here, send, recv):
        return [
            remote(src_of(at), dst.at[turn, here], send.at[kind, turn, step], recv.at[kind, turn, here], peer)
            for step, (peer, at) in enumerate(others)
        ]

    def pull(kind, turn, others, src_of, dst, send, recv):
        return [
            remote(src_of(at), dst.at[turn, at], send.at[kind, turn, step], recv.at[kind, turn, at], peer)
            for step, (peer, at) in enumerate(others)
        ]

    def start_all(*args):
        for copy in push(*args):
            copy.start()

    def wait_received(*args):
        for copy in pull(*args):
            copy.wait_recv()

    def wait_sent(*args):
        for copy in pull(*args):
            copy.wait_send()

    def coarse_of(scaled):
        high, low = halves(scaled)
        return dot_nt(basis[:32, :scaled.shape[1]], jnp.concatenate([high, low], axis=0))

    def pack(out):
        value = out[:16] + flip(out[:16]) + out[16:]
        return jnp.where(left_half, value[:8], flip(value[8:]))

    def start_gather(turn, own):
        gather_own[...] = own
        gather[turn, col] = own
        start_all(0, turn, flat_others, lambda at: gather_own, gather, col, flat_send, flat_recv)

    def start_spread(turn):
        wait_received(0, turn, flat_others, lambda at: gather_own, gather, flat_send, flat_recv)
        packed = gather[turn]
        turned = flip(packed)
        both = jnp.concatenate(
            [jnp.where(left_half, packed, turned), jnp.where(left_half, turned, packed)], axis=1
        ).reshape(plane * 16, wide)
        high = both.astype(BF16).astype(F32)
        right = jnp.where(left_half, high, both - high).astype(BF16)
        out = dot(coarse_cat[...], right)
        lines = planes * 16
        value = out[:lines] + flip(out[:lines]) + out[lines:]
        value = value.reshape(planes, 2, 8, wide)
        spread_out[...] = jnp.where(left_half, value[:, 0], flip(value[:, 1]))
        spread[turn, deep] = spread_out[deep]
        start_all(0, turn, deep_others, lambda at: spread_out.at[at], spread, deep, deep_send, deep_recv)
        wait_sent(0, turn, flat_others, lambda at: gather_own, gather, flat_send, flat_recv)

    def wait_spread(turn):
        wait_sent(0, turn, deep_others, lambda at: spread_out.at[at], spread, deep_send, deep_recv)
        wait_received(0, turn, deep_others, lambda at: spread_out.at[at], spread, deep_send, deep_recv)
        return jnp.sum(spread[turn], axis=0)

    def coarse_stack(packed):
        both = jnp.concatenate([packed, flip(packed)], axis=0)
        high = both.astype(BF16).astype(F32)
        return jnp.concatenate([high, high, both - high, jnp.zeros_like(high)], axis=0)

    def coarse_rows(*packed):
        return jnp.concatenate([coarse_stack(one) for one in packed], axis=0).T[:cases].astype(BF16)

    def row_sum(value):
        part = value[:, :128]
        for block in range(128, ndof, 128):
            part = part + value[:, block:block + 128]
        part = jnp.sum(part.T, axis=0, keepdims=True)
        return jnp.concatenate([part, part], axis=1)

    def as_column(scalar_row):
        return jnp.broadcast_to(scalar_row, (8, wide)).T[:cases, :1]

    def start_sums(turn, parts):
        own = jnp.concatenate(parts, axis=1)
        sums_own[...] = own
        sums[turn, col] = own
        start_all(1, turn, flat_others, lambda at: sums_own, sums, col, flat_send, flat_recv)

    def lift_sums(turn):
        wait_received(1, turn, flat_others, lambda at: sums_own, sums, flat_send, flat_recv)
        own = jnp.sum(sums[turn], axis=0)
        tops_own[...] = own
        tops[turn, deep] = own
        start_all(1, turn, deep_others, lambda at: tops_own, tops, deep, deep_send, deep_recv)
        wait_sent(1, turn, flat_others, lambda at: sums_own, sums, flat_send, flat_recv)

    def wait_sums(turn):
        wait_sent(1, turn, deep_others, lambda at: tops_own, tops, deep_send, deep_recv)
        wait_received(1, turn, deep_others, lambda at: tops_own, tops, deep_send, deep_recv)
        total = jnp.sum(tops[turn], axis=0)
        return total[:, :wide], total[:, wide:2 * wide], total[:, 2 * wide:]

    tall = 256

    def turn(which, start, stop):
        def block(step, carry):
            here = pl.ds(pl.multiple_of(step * tall, tall), tall)
            high, low = halves(raw[which, here, :])
            both = dot_nt(jnp.concatenate([high, low], axis=0), perm[start:stop, :]).astype(BF16)
            turned_hi[here, start:stop] = both[:tall]
            turned_lo[here, start:stop] = both[tall:]
            return carry

        lax.fori_loop(0, ndof // tall, block, 0)

    def settle(out_hi, out_lo, start, stop, begin, end):
        def block(step, carry):
            here = pl.ds(pl.multiple_of(step * tall, tall), tall)
            pick = perm[here, :]
            out_hi[here, start:stop] = dot(pick, turned_hi[:, start:stop]).astype(BF16)
            out_lo[here, start:stop] = dot(pick, turned_lo[:, start:stop]).astype(BF16)
            return carry

        lax.fori_loop(begin, end, block, 0)

    start_faces(1, first)
    for step, (peer, at) in enumerate(deep_others):
        remote(
            coarse_hbm.at[:, coarse_cols(at)], coarse_raw.at[deep], deep_send.at[2, 0, step], deep_recv.at[2, 0, deep], peer
        ).start()
    sol_ref[...] = jnp.zeros_like(sol_ref)
    direction_ref[...] = jnp.zeros_like(direction_ref)
    image_ref[...] = jnp.zeros_like(image_ref)
    scalars[...] = jnp.ones_like(scalars)

    taken = dot(jnp.ones((16, shared), BF16), perm[:shared, :])[:8]
    free = (1.0 - taken).astype(BF16)
    rank = jnp.zeros((8, ndof), F32)
    for block in range(0, ndof, 128):
        before = jnp.where(iota((128, ndof), 0) + block < iota((128, ndof), 1), 1.0, 0.0).astype(BF16)
        rank = rank + dot(free[:, block:block + 128], before)
    place = jnp.where(taken[:1] > 0.5, -1.0, rank[:1]).astype(jnp.int32)
    for block in range(0, ndof - shared, 128):
        hit = place == iota((128, ndof), 0) + block
        perm[shared + block:shared + block + 128, :] = jnp.where(hit, 1.0, 0.0).astype(BF16)
    rest = three(dot_nt(loads_cat, perm[shared:, :]), cases)
    basis_own = three(dot_nt(jnp.concatenate(thirds(basis_ref[0]), axis=0), perm[...]), 16)
    for block in range(faces):
        side_basis[0, block] = basis_own[:, block * width:(block + 1) * width]
    start_sides(2)
    side_mix[...] = jnp.zeros_like(side_mix)
    side_wide[...] = jnp.zeros_like(side_wide)
    basis_hi, basis_lo = halves(basis_own)
    basis[...] = jnp.concatenate(
        [basis_hi, basis_lo, basis_hi, basis_lo, basis_hi, jnp.zeros_like(basis_hi)], axis=0
    )
    load_neum.wait()
    turn(0, 0, ndof)
    resid = jnp.concatenate([first + wait_faces(1), rest], axis=1)
    start_gather(0, pack(coarse_of(weight * resid)))
    res_ref[...] = resid
    load_coarse.wait()
    for receive in (False, True):
        for step, (peer, at) in enumerate(deep_others):
            copy = remote(
                coarse_hbm.at[:, coarse_cols(at)], coarse_raw.at[at], deep_send.at[2, 0, step], deep_recv.at[2, 0, at], peer
            )
            if receive:
                copy.wait_recv()
            else:
                copy.wait_send()
    coarse_hi, coarse_lo = halves(coarse_raw[...].reshape(planes * 16, plane * 16))
    coarse_cat[...] = jnp.concatenate([coarse_hi, coarse_lo], axis=0)
    settle(neum_hi, neum_lo, 0, ndof, 0, ndof // tall)
    start_spread(0)
    local_ref[...] = product(weight * res_ref[...], neum_hi, neum_lo, 0, ndof)
    start_faces(0, weight[:, :shared] * local_ref[:, :shared])
    wait_sides(2)
    for block in range(faces):
        near_basis = side_basis[1, block] * jnp.where(live[:, block * width:(block + 1) * width], 0.5, 0.0)
        high, low = halves(near_basis)
        at = slice(block * width, (block + 1) * width)
        side_mix[32 * block:32 * (block + 1), at] = jnp.concatenate([high, low], axis=0)
        side_wide[64 * block:64 * (block + 1), at] = jnp.concatenate([high, low, high, jnp.zeros_like(high)], axis=0)
    load_stiff.wait()
    turn(1, 0, shared)
    coarse_first = wait_spread(0)
    coarse_state[0] = coarse_first
    for block in range(faces):
        side_out[0, block] = coarse_first
    start_sides(0)
    coarse_state[1] = jnp.zeros_like(coarse_state[1])
    slope_ref[...] = jnp.zeros_like(slope_ref)
    edge_ref[0] = wait_faces(0)
    edge_ref[1] = jnp.zeros_like(edge_ref[1])

    def unturn(one, two):
        both = three(dot(jnp.concatenate(thirds(jnp.concatenate([one, two], axis=0)), axis=0), perm[...]), 2 * cases)
        return [both[:cases], both[cases:]]

    def iterate(step, last):
        now, later = (step % 2, (step + 1) % 2) if last else (lax.rem(step, 2), lax.rem(step + 1, 2))
        coarse_part = coarse_rows(coarse_state[0])
        half_sol = weight * (local_ref[...] + dot(coarse_part, basis[32:, :]))
        rz_part = row_sum(half_sol * res_ref[...])

        if not last:
            @pl.when(step == 0)
            def _():
                settle(stiff_hi, stiff_lo, 0, shared, 0, ndof // tall)

        wait_sides(0)
        incoming = edge_ref[0] + dot(coarse_rows(*[side_in[0, block] for block in range(faces)]), side_wide[...])
        precond = add_faces(half_sol, incoming)
        near = product(precond, stiff_hi, stiff_lo, 0, shared)
        if not last:
            high, low = halves(near)
            mixed = dot_nt(side_mix[...], jnp.concatenate([high, low], axis=0))
            for block in range(faces):
                side_out[1, block] = pack(mixed[32 * block:32 * (block + 1)])
            start_sides(1)
        start_faces(1, near)

        if not last:
            @pl.when(step == 0)
            def _():
                turn(1, shared, ndof)
                settle(stiff_hi, stiff_lo, shared, ndof, 0, ndof // tall)

        image = jnp.concatenate([near, product(precond, stiff_hi, stiff_lo, shared, ndof)], axis=1)
        zz_part = row_sum(precond * image)
        zq_part = row_sum(weight * precond * image_ref[...])
        start_sums(now, [rz_part, zz_part, zq_part])
        if last:
            kept = unturn(sol_ref[...], precond) + unturn(direction_ref[...], res_ref[...])
            image = add_faces(image, wait_faces(1))
        else:
            coarse_own = pack(coarse_of(weight * image))
            wait_sides(1)
            start_gather(later, coarse_own + jnp.sum(side_in[1], axis=0))
            image = add_faces(image, wait_faces(1))
            local_image = product(weight * image, neum_hi, neum_lo, 0, ndof)
            start_faces(0, weight[:, :shared] * local_image[:, :shared])
        lift_sums(now)
        if last:
            kept = kept + unturn(image, image_ref[...])
        else:
            start_spread(later)
        rz, zz, zq = wait_sums(now)
        beta = jnp.where(step > 0, rz / scalars[0:1], 0.0)
        denom = zz + beta * (2.0 * zq) + beta * (beta * jnp.where(step > 0, scalars[1:2], 0.0))
        alpha = rz / denom
        slope, length = as_column(beta), as_column(alpha)
        if last:
            sol_out[...] = kept[0] + length * (kept[1] + slope * kept[2])
            res_out[...] = kept[3] - length * (kept[4] + slope * kept[5])
            return
        direction = precond + slope * direction_ref[...]
        image = image + slope * image_ref[...]
        resid = res_ref[...] - length * image
        sol_ref[...] = sol_ref[...] + length * direction
        res_ref[...] = resid
        direction_ref[...] = direction
        image_ref[...] = image
        scalars[0:1] = rz
        scalars[1:2] = denom
        local_image = local_image + slope * slope_ref[...]
        slope_ref[...] = local_image
        local_ref[...] = local_ref[...] - length * local_image
        edge_image = wait_faces(0) + slope * edge_ref[1]
        edge_ref[1] = edge_image
        edge_ref[0] = edge_ref[0] - length * edge_image
        coarse_image = wait_spread(later) + beta * coarse_state[1]
        coarse_next = coarse_state[0] - alpha * coarse_image
        for block in range(faces):
            side_out[0, block] = coarse_next
        start_sides(0)
        coarse_state[1] = coarse_image
        coarse_state[0] = coarse_next

    def body(step, carry):
        iterate(step, False)
        return carry

    lax.fori_loop(0, ITERS - 1, body, 0)
    iterate(ITERS - 1, True)


def hand_over(sol_ref, res_ref, sol_out, res_out):
    sol_out[0] = sol_ref[...]
    res_out[0] = res_ref[...]


def local(sizes, cycle, stiffness, neumann_inv, coarse_basis, coarse_inv, loads, face_index, face_len):
    cases, ndof = loads.shape[1:]
    faces, width = face_index.shape[1:]
    planes, plane = sizes
    wide = 2 * cases
    anywhere = pl.BlockSpec(memory_space=pl.ANY)
    inside = pl.BlockSpec(memory_space=pltpu.VMEM)
    square = pltpu.VMEM((ndof, ndof), BF16)
    plain = pltpu.VMEM((cases, ndof), F32)
    whole = jax.ShapeDtypeStruct((1, cases, ndof), F32)
    flat = jax.ShapeDtypeStruct((cases, ndof), F32)
    results = pl.pallas_call(
        functools.partial(kernel, sizes, cycle),
        out_shape=(flat, flat),
        in_specs=[anywhere, anywhere, inside, anywhere, inside, inside, pl.BlockSpec(memory_space=pltpu.SMEM)],
        out_specs=(inside, inside),
        scratch_shapes=[
            pltpu.VMEM((2, ndof, ndof), F32),
            square, square, square, square, square, square, square,
            pltpu.VMEM((96, ndof), BF16),
            plain, plain,
            pltpu.VMEM((planes, 16, plane * 16), F32),
            pltpu.VMEM((2 * planes * 16, plane * 16), BF16),
            pltpu.VMEM((cases, ndof), F32),
            pltpu.VMEM((cases, ndof), F32),
            pltpu.VMEM((cases, ndof), F32),
            plain,
            pltpu.VMEM((2, cases, faces * width), F32),
            pltpu.VMEM((8, wide), F32),
            pltpu.VMEM((2, 8, wide), F32),
            pltpu.VMEM((2, faces, cases, width), F32),
            pltpu.VMEM((2, faces, cases, width), F32),
            pltpu.VMEM((2, plane, 8, wide), F32),
            pltpu.VMEM((8, wide), F32),
            pltpu.VMEM((2, planes, 8, wide), F32),
            pltpu.VMEM((planes, 8, wide), F32),
            pltpu.VMEM((2, plane, 1, 3 * wide), F32),
            pltpu.VMEM((1, 3 * wide), F32),
            pltpu.VMEM((2, planes, 1, 3 * wide), F32),
            pltpu.VMEM((1, 3 * wide), F32),
            pltpu.VMEM((2, faces, 16, width), F32),
            pltpu.VMEM((32 * faces, faces * width), BF16),
            pltpu.VMEM((64 * faces, faces * width), BF16),
            pltpu.VMEM((2, faces, 8, wide), F32),
            pltpu.VMEM((2, faces, 8, wide), F32),
            pltpu.SemaphoreType.DMA((3,)),
            pltpu.SemaphoreType.DMA((2, faces)),
            pltpu.SemaphoreType.DMA((2, faces)),
            pltpu.SemaphoreType.DMA((3, faces)),
            pltpu.SemaphoreType.DMA((3, faces)),
            pltpu.SemaphoreType.DMA((2, 2, plane)),
            pltpu.SemaphoreType.DMA((2, 2, plane)),
            pltpu.SemaphoreType.DMA((3, 2, planes)),
            pltpu.SemaphoreType.DMA((3, 2, planes)),
        ],
        compiler_params=pltpu.CompilerParams(
            collective_id=0, has_side_effects=True, vmem_limit_bytes=56 * 1024 * 1024
        ),
        name="solve",
    )(stiffness, neumann_inv, coarse_basis, coarse_inv, loads, face_index, face_len)
    return pl.pallas_call(
        hand_over, out_shape=(whole, whole), in_specs=[inside] * 2, out_specs=(inside, inside), name="hand_over"
    )(*results)


def solution(mesh, plane=PLANE, cycle=CYCLE):
    subs = mesh.shape["sub"]
    placed = (
        P("sub", None, None),
        P("sub", None, None),
        P("sub", None, None),
        P("sub", None),
        P("sub", None, None),
        P("sub", None, None),
        P("sub", None),
    )
    return jax.shard_map(
        functools.partial(local, (subs // plane, plane), cycle),
        mesh=mesh,
        in_specs=placed,
        out_specs=(P("sub", None, None), P("sub", None, None)),
        check_vma=False,
    )
```
